128 devices in a mesh: rx: 8 (over x, core), ry: 16 (over z, y).
Axes of the slice: x: 4, y: 4, z: 4, core: 2. Of those that a mesh axis runs over, the one named last changes fastest.
Arguments:
- noisy_input: bfloat16 [147456, 12, 128], P(('rx', 'ry')), may hold values from -6 to 6
- adjacency: bfloat16 [1152, 6, 128, 128], P(('rx', 'ry')), may hold values from -0.21875 to 0.21875
- neighbours: int32 [1152, 6], P(('rx', 'ry')), may hold values from 0 to 8, as said below
- norm_gain: float32 [128], replicated, may hold values from 0.1 to 1.9
- w_mix: bfloat16 [128, 128], replicated, may hold values from -0.5 to 0.5
- pool_weight: bfloat16 [147456], P(('rx', 'ry')), may hold values from 0.049804688 to 0.29882812
- cluster: int32 [147456], P(('rx', 'ry')), may hold values from 0 to 143, as said below
- owner_ids: int32 [18432, 1], P(('rx', 'ry')), may hold values from 0 to 127; in each aligned block of 144 rows (0 to 143, 144 to 287, ...) at most 2 rows name the same one
- w_coarse: bfloat16 [128, 128], replicated, may hold values from -0.5 to 0.5
- w_region: bfloat16 [128, 128], replicated, may hold values from -0.5 to 0.5
- w_out: bfloat16 [128, 128], replicated, may hold values from -0.5 to 0.5
Outputs:
- denoised: bfloat16 [147456, 12, 128], P(('rx', 'ry'))
The draws below stay inside these ranges and needn't reach their ends.
Inputs may be any that keep to these rules, and one draw needn't show every extreme that they name: `neighbours`: the 6 codes of one block are different. `cluster`: among the 1152 nodes of one device's square each value is taken by exactly 8 nodes. `owner_ids`: in each aligned block of 144 rows no value is named by more than 2 rows, and one value is named by exactly 2 rows in some or all blocks; every value is named by some row.
All inputs are finite; a program needn't handle non-finite values.
Results may differ from the reference program's by a relative error of at most 0.015.
Values may be sent and summed in bfloat16 or wider, within the bound.
No kernel may reach another device: no remote copies, remote signals or barrier semaphores. Data moves between devices by JAX's collectives and lax.ppermute only.
A program may use at most 128 MiB of HBM per device.

```python
import math
import jax
import jax.numpy as jnp
import numpy as np
from jax import lax

GB = 3
BLK = 128
NB = 6
STEPS = 12
C = 128
ROWS_DEV = 1152
CROWS_DEV = 144
CAP = 2
NODES = 147456
BLOCKS = 1152
COARSE = 18432
N_RX = 8
N_RY = 16
DEVICES = 128


def draw_neighbours(key, part):
    ranking = jax.random.randint(key, (BLOCKS, 9), 0, 1 << 20) * 16 + jnp.arange(9, dtype=jnp.int32)[None, :]
    ordering = jnp.argsort(ranking, axis=1, stable=True)
    return ordering[:, :NB].astype(jnp.int32)


def shuffle_one(subkey):
    return jax.random.permutation(subkey, ROWS_DEV)


def draw_cluster(key, part):
    subkeys = jax.random.split(key, NODES // ROWS_DEV)
    shuffled = jax.vmap(shuffle_one)(subkeys)
    return (shuffled // 8).reshape(NODES).astype(jnp.int32)


def block_levels(key, extent, pieces, least, high):
    factor_of, own = 1.0, jax.random.fold_in(key, 6)
    for dim, blocks in pieces:
        draws = jnp.exp(jax.random.uniform(jax.random.fold_in(own, dim), (blocks,), jnp.float32, least / len(pieces), high / len(pieces)))
        factor_of = factor_of * jnp.repeat(draws, extent[dim] // blocks).reshape([-1 if axis == dim else 1 for axis in range(len(extent))])
    return factor_of


def shared_out(rng, own, number, rows, count, top, limit, slope):
    sequence = jax.random.permutation(rng, count)
    heavy_load, common = shares(count, rows * top, limit, slope, True), shares(count, rows * top, limit, slope, False)
    places = jnp.arange(count)

    def named(tallies, offset_by):
        used = int((tallies > 0).sum())
        fixed = max(1, used // 4)
        passed = fixed + (places - fixed + offset_by * (used - fixed)) % max(1, count - fixed)
        return jnp.zeros((count,), jnp.int32).at[sequence[jnp.where(places < fixed, places, passed)]].set(jnp.asarray(tallies, jnp.int32))

    tallies = jnp.where(number % 4 == 0, named(heavy_load, number // 4), named(common, number - number // 4 - 1))
    mixed = jax.random.permutation(jax.random.fold_in(own, 3), count)
    source_of, sink = mixed[0:count // 2 * 2:2], mixed[1:count // 2 * 2:2]
    room = jnp.minimum(tallies[source_of] - 1, limit - tallies[sink]) // 2
    room = jnp.where((source_of == sequence[0]) | (sink == sequence[0]) | (tallies[sink] == 0), 0, jnp.maximum(room, 0))
    passed = jax.random.randint(jax.random.fold_in(own, 4), (count // 2,), 0, 1 << 20) % (room + 1)
    tallies = tallies.at[source_of].add(-passed).at[sink].add(passed)
    members = jnp.searchsorted(jnp.cumsum(tallies), jnp.arange(rows * top), side="right").astype(jnp.int32)
    grid = members.reshape(top, rows).T
    grid = grid[jax.random.permutation(jax.random.fold_in(own, 1), rows)]
    offset_by = jax.random.randint(jax.random.fold_in(own, 2), (rows, 1), 0, top)
    return jnp.take_along_axis(grid, (jnp.arange(top)[None, :] + offset_by) % top, axis=1)


def shares(number_of, total, limit, skew, full):
    loads = [(1 << 20) // math.isqrt(standing ** skew) + 1 for standing in range(1, number_of + 1)]
    largest = limit if full else min(limit, max(-(-total // number_of), total * loads[0] // sum(loads)))
    least = 1 if total - largest >= number_of - 1 else 0
    holding, surplus = [largest] + [least] * (number_of - 1), total - largest - least * (number_of - 1)
    while surplus > 0:
        free = [i for i in range(1, number_of) if holding[i] < largest] or [i for i in range(1, number_of) if holding[i] < limit]
        mass, budget = sum([loads[i] for i in free]), surplus
        for i in free:
            addition = min(limit - holding[i], max(1, budget * loads[i] // mass), surplus)
            holding[i] = holding[i] + addition
            surplus = surplus - addition
    return np.array(holding)


def gaussian(key, shape, width, limit, cuts=(), held_as=jnp.bfloat16):
    loudness = block_levels(key, shape, cuts, -0.22, 0.18) if cuts else 1.0
    drawn = jax.random.normal(key, shape, jnp.float32) * width * loudness
    return jnp.minimum(jnp.maximum(drawn, -limit), limit).astype(held_as)


def setup_inputs(seed: int = 0) -> dict:
    splits = jax.random.split(jax.random.key(seed), 12)
    noisy_input = gaussian(splits[0], (NODES, STEPS, C), 1.0, 6.0, ((0, 128),))
    adjacency = gaussian(splits[1], (BLOCKS, NB, BLK, BLK), (NB * BLK) ** -0.5, 0.21875, ((0, 128),))
    neighbours = draw_neighbours(jax.random.fold_in(splits[11], 71), 0)
    norm_gain = jnp.clip(1.0 + 0.18 * jax.random.normal(splits[3], (C,), jnp.float32), 0.1, 1.9)
    w_mix = gaussian(splits[4], (C, C), C ** -0.5, 0.5)
    pool_weight = jnp.clip(jnp.exp(math.log(0.29882812) - 1.7917595 * jax.random.uniform(splits[5], (NODES,), jnp.float32) ** block_levels(splits[5], (NODES,), ((0, 128),), -0.2, 0.2)), 0.049804688, 0.29882812).astype(jnp.bfloat16)
    cluster = draw_cluster(jax.random.fold_in(splits[11], 71), 0)
    owner_ids_keys = jax.random.split(jax.random.fold_in(splits[7], 1), COARSE // CROWS_DEV)
    owner_ids_turns = jax.random.permutation(jax.random.fold_in(splits[7], 3), COARSE // CROWS_DEV)
    owner_ids = jax.vmap(lambda own, number: shared_out(jax.random.fold_in(splits[7], 2), own, number, CROWS_DEV, DEVICES, 1, CAP, 2))(owner_ids_keys, owner_ids_turns).reshape((COARSE, 1))
    w_coarse = gaussian(splits[8], (C, C), C ** -0.5, 0.5)
    w_region = gaussian(splits[9], (C, C), C ** -0.5, 0.5)
    w_out = gaussian(splits[10], (C, C), C ** -0.5, 0.5)
    return dict(noisy_input=noisy_input, adjacency=adjacency, neighbours=neighbours, norm_gain=norm_gain, w_mix=w_mix, pool_weight=pool_weight, cluster=cluster, owner_ids=owner_ids, w_coarse=w_coarse, w_region=w_region, w_out=w_out)


def diffuse(values_in, adjacency, offsets):
    features = STEPS * C
    grid_blocks = values_in.reshape(N_RX, N_RY, GB, GB, BLK, features)
    grid_blocks = grid_blocks.transpose(0, 2, 1, 3, 4, 5).reshape(N_RX * GB, N_RY * GB, BLK, features)
    padded = jnp.pad(grid_blocks, ((1, 1), (1, 1), (0, 0), (0, 0)))
    local_weights = adjacency.reshape(DEVICES, GB * GB, NB, BLK, BLK)
    local_offsets = offsets.reshape(DEVICES, GB * GB, NB)
    positions = jnp.arange(GB * GB, dtype=jnp.int32)

    def one_device(carried):
        device_id, weights, offset_codes = carried
        first_row = device_id // N_RY * GB
        first_col = device_id % N_RY * GB
        row_at = first_row + (positions // GB)[:, None] + offset_codes // 3
        col_at = first_col + (positions % GB)[:, None] + offset_codes % 3
        gathered = padded[row_at, col_at]
        return jnp.einsum('bkij,bkjf->bif', weights.astype(jnp.float32), gathered.astype(jnp.float32))
    summed = lax.map(one_device, (jnp.arange(DEVICES, dtype=jnp.int32), local_weights, local_offsets))
    return summed.reshape(NODES, STEPS, C)

def reference(noisy_input, adjacency, neighbours, norm_gain, w_mix, pool_weight, cluster, owner_ids, w_coarse, w_region, w_out):
    diffused = diffuse(noisy_input, adjacency, neighbours).astype(jnp.bfloat16)
    scaled = diffused.astype(jnp.float32)
    mean_square = lax.optimization_barrier(jnp.mean(scaled * scaled, axis=-1, keepdims=True))
    normed = (scaled * lax.rsqrt(mean_square + 1e-06) * norm_gain).astype(jnp.bfloat16)
    mixed = jnp.dot(normed.reshape(-1, C), w_mix, preferred_element_type=jnp.float32).reshape(NODES, STEPS, C)
    encoded = (noisy_input.astype(jnp.float32) + jax.nn.silu(mixed)).astype(jnp.bfloat16)
    coarse_index = jnp.arange(NODES, dtype=jnp.int32) // ROWS_DEV * CROWS_DEV + cluster
    weighted = pool_weight.astype(jnp.float32)[:, None, None] * encoded.astype(jnp.float32)
    pooled = jax.ops.segment_sum(weighted, coarse_index, COARSE).astype(jnp.bfloat16)
    owners = owner_ids[:, 0]
    lifted = jax.nn.silu(jnp.dot(pooled.reshape(-1, C), w_coarse, preferred_element_type=jnp.float32))
    lifted = lifted.astype(jnp.bfloat16).reshape(COARSE, STEPS, C)
    region_sum = jax.ops.segment_sum(lifted.astype(jnp.float32), owners, DEVICES)
    region = (region_sum / float(CROWS_DEV)).astype(jnp.bfloat16)
    reach = jnp.dot(region.reshape(-1, C), w_region, preferred_element_type=jnp.float32).reshape(DEVICES, STEPS, C)
    refined = (pooled.astype(jnp.float32) + lifted.astype(jnp.float32) + reach[owners]).astype(jnp.bfloat16)
    decoder_in = (encoded.astype(jnp.float32) + refined[coarse_index].astype(jnp.float32)).astype(jnp.bfloat16)
    second = diffuse(decoder_in, adjacency, neighbours).astype(jnp.bfloat16)
    output = jnp.dot(second.reshape(-1, C), w_out, preferred_element_type=jnp.float32).reshape(NODES, STEPS, C)
    return (decoder_in.astype(jnp.float32) + jax.nn.silu(output)).astype(jnp.bfloat16)
```

```python
import functools
import jax
import jax.numpy as jnp
from jax import lax
from jax.experimental import pallas as pl
from jax.experimental.pallas import tpu as pltpu
from jax.sharding import PartitionSpec as P

GB, BLK, NB, C = 3, 128, 6, 128
CHUNKS = (12,)
EXT = GB + 2
ROWS = GB * GB * BLK
bf16, f32 = jnp.bfloat16, jnp.float32


def fill(ext, own, yl, yr, xu, xd, cu, cd, pair):
    for s in range(pair):
        lanes = slice(s * C, (s + 1) * C)

        def put(row, col, block):
            e = (row * EXT + col) * BLK
            ext[e : e + BLK, lanes] = block

        for a in range(GB):
            for b in range(GB):
                k = (a * GB + b) * BLK
                put(a + 1, b + 1, own[s, k : k + BLK, :])
            put(a + 1, 0, yl[s, a * BLK : (a + 1) * BLK, :])
            put(a + 1, EXT - 1, yr[s, a * BLK : (a + 1) * BLK, :])
            put(0, a + 1, xu[s, a * BLK : (a + 1) * BLK, :])
            put(EXT - 1, a + 1, xd[s, a * BLK : (a + 1) * BLK, :])
        for e, col in enumerate((0, EXT - 1)):
            put(0, col, cu[s, e * BLK : (e + 1) * BLK, :])
            put(EXT - 1, col, cd[s, e * BLK : (e + 1) * BLK, :])


def ext_row(codes, j, n):
    code = codes[j * NB + n]
    e = (j // GB + code // 3) * EXT + j % GB + code % 3
    return pl.ds(pl.multiple_of(e * BLK, BLK), BLK)


def silu(v):
    return v / (1.0 + jnp.exp(-v))


def dot(a, b):
    return jnp.dot(a, b, preferred_element_type=f32)


def encode_kernel(pair, codes, own, yl, yr, xu, xd, cu, cd, adj, gain, w_mix, w_coarse, pool, unpool, spread,
                  d1, dl, dr, du, dd, part, ext, enc):
    fill(ext, own, yl, yr, xu, xd, cu, cd, pair)
    for j in range(GB * GB):
        weights = jnp.concatenate([adj[j, n] for n in range(NB)], axis=1)
        feats = jnp.concatenate([ext[ext_row(codes, j, n), :] for n in range(NB)], axis=0)
        diffused = dot(weights, feats).astype(bf16).astype(f32)
        rows = slice(j * BLK, (j + 1) * BLK)
        for s in range(pair):
            lanes = slice(s * C, (s + 1) * C)
            v = diffused[:, lanes]
            ms = jnp.mean(v * v, axis=1, keepdims=True)
            normed = (v * lax.rsqrt(ms + 1e-6) * gain[...]).astype(bf16)
            mixed = dot(normed, w_mix[...])
            enc[rows, lanes] = (own[s, rows, :].astype(f32) + silu(mixed)).astype(bf16)
    pooled = dot(pool[...], enc[...]).astype(bf16)
    refined = []
    lifts = []
    for s in range(pair):
        lanes = slice(s * C, (s + 1) * C)
        lifted = silu(dot(pooled[:, lanes], w_coarse[...])).astype(bf16)
        lifts.append(lifted)
        refined.append((pooled[:, lanes].astype(f32) + lifted.astype(f32)).astype(bf16))
    part[...] = dot(spread[...], jnp.concatenate(lifts, axis=1)).astype(bf16)
    refined = jnp.concatenate(refined, axis=1)
    for j in range(GB * GB):
        rows = slice(j * BLK, (j + 1) * BLK)
        back = (enc[rows, :].astype(f32) + dot(unpool[rows, :], refined)).astype(bf16)
        a, b = j // GB, j % GB
        for s in range(pair):
            v = back[:, s * C : (s + 1) * C]
            d1[s, rows, :] = v
            if b == 0:
                dl[s, a * BLK : (a + 1) * BLK, :] = v
            if b == GB - 1:
                dr[s, a * BLK : (a + 1) * BLK, :] = v
            if a == 0:
                du[s, b * BLK : (b + 1) * BLK, :] = v
            if a == GB - 1:
                dd[s, b * BLK : (b + 1) * BLK, :] = v


def decode_kernel(pair, codes, own, yl, yr, xu, xd, cu, cd, adj, mown, region, w_region, w_out, hot, *rest):
    out, ext = rest[-2], rest[-1]
    fill(ext, own, yl, yr, xu, xd, cu, cd, pair)
    reach = jnp.concatenate(
        [dot(region[:, s * C : (s + 1) * C], w_region[...]).astype(bf16) for s in range(pair)], axis=1)
    for j in range(GB * GB):
        weights = jnp.concatenate([adj[j, n] for n in range(NB)], axis=1)
        feats = jnp.concatenate([ext[ext_row(codes, j, n), :] for n in range(NB)], axis=0)
        second = (dot(weights, feats) + dot(mown[j], reach)).astype(bf16)
        rows = slice(j * BLK, (j + 1) * BLK)
        extra = dot(hot[rows, :], reach)
        for s in range(pair):
            lanes = slice(s * C, (s + 1) * C)
            dec = (own[s, rows, :].astype(f32) + extra[:, lanes]).astype(bf16).astype(f32)
            out[s, rows, :] = (dec + silu(dot(second[:, lanes], w_out[...]))).astype(bf16)


def owners_kernel(codes, adj, owners, mown, hot):
    lane_ids = lax.broadcasted_iota(jnp.int32, (C, BLK), 0)
    for e in range(EXT * EXT):
        row = owners[e : e + 1, :].astype(f32).astype(jnp.int32) - 1
        hot[e * BLK : (e + 1) * BLK, :] = (lane_ids == row).astype(f32).astype(bf16)
    for j in range(GB * GB):
        acc = jnp.zeros((BLK, C), f32)
        for n in range(NB):
            acc += lax.dot_general(adj[j, n], hot[ext_row(codes, j, n), :], (((1,), (1,)), ((), ())),
                                   preferred_element_type=f32)
        mown[j] = acc.astype(bf16)


def whole(shape):
    return pl.BlockSpec(shape, lambda p, *_: (0,) * len(shape))


def steps_of(pair, rows, first=0):
    return pl.BlockSpec((pair, rows, C), lambda p, *_: (p + first // pair, 0, 0))


PARAMS = pltpu.CompilerParams(vmem_limit_bytes=48 << 20, dimension_semantics=("arbitrary",))


def encode(codes, x, first, nt, yl, yr, xu, xd, cu, cd, adj, gain, w_mix, w_coarse, pool, unpool, spread, pair=2):
    side = GB * BLK
    crows, owners = pool.shape[0], spread.shape[0]
    sds = lambda *s: jax.ShapeDtypeStruct(s, bf16)
    return pl.pallas_call(
        functools.partial(encode_kernel, pair),
        grid_spec=pltpu.PrefetchScalarGridSpec(
            num_scalar_prefetch=1, grid=(nt // pair,),
            in_specs=[steps_of(pair, ROWS, first)] + [steps_of(pair, side)] * 4 + [steps_of(pair, 2 * BLK)] * 2
            + [whole(adj.shape), whole((1, C)), whole((C, C)), whole((C, C)), whole(pool.shape), whole(unpool.shape), whole(spread.shape)],
            out_specs=[steps_of(pair, ROWS)] + [steps_of(pair, side)] * 4
            + [pl.BlockSpec((owners, pair * C), lambda p, *_: (0, p))],
            scratch_shapes=[pltpu.VMEM((EXT * EXT * BLK, pair * C), bf16), pltpu.VMEM((ROWS, pair * C), bf16)]),
        out_shape=[sds(nt, ROWS, C)] + [sds(nt, side, C)] * 4 + [sds(owners, nt * C)],
        compiler_params=PARAMS,
        name="encode",
        cost_estimate=pl.CostEstimate(flops=nt * ROWS * C * 2 * (NB * BLK + C + 3 * crows), bytes_accessed=nt * ROWS * C * 2 * 5, transcendentals=nt * ROWS * C),
    )(codes, x, yl, yr, xu, xd, cu, cd, adj, gain, w_mix, w_coarse, pool, unpool, spread)


def decode(codes, d1, first, nt, total, yl, yr, xu, xd, cu, cd, adj, mown, region, w_region, w_out, hot, prev=None, pair=2):
    side = GB * BLK
    owners = region.shape[0]
    args = [codes, d1, yl, yr, xu, xd, cu, cd, adj, mown, region, w_region, w_out, hot]
    specs = ([steps_of(pair, ROWS)] + [steps_of(pair, side)] * 4 + [steps_of(pair, 2 * BLK)] * 2
             + [whole(adj.shape), whole(mown.shape), pl.BlockSpec((owners, pair * C), lambda p, *_: (0, p)),
                whole((C, C)), whole((C, C)), whole(hot.shape)])
    alias = {}
    if prev is not None:
        alias = {len(args): 0}
        args.append(prev)
        specs.append(pl.BlockSpec(memory_space=pl.ANY))
    return pl.pallas_call(
        functools.partial(decode_kernel, pair),
        grid_spec=pltpu.PrefetchScalarGridSpec(
            num_scalar_prefetch=1, grid=(nt // pair,), in_specs=specs,
            out_specs=steps_of(pair, ROWS, first),
            scratch_shapes=[pltpu.VMEM((EXT * EXT * BLK, pair * C), bf16)]),
        out_shape=jax.ShapeDtypeStruct((total, ROWS, C), bf16),
        input_output_aliases=alias,
        compiler_params=PARAMS,
        name="decode",
        cost_estimate=pl.CostEstimate(flops=nt * ROWS * C * 2 * (NB * BLK + 3 * C), bytes_accessed=nt * ROWS * C * 2 * 5, transcendentals=nt * ROWS * C),
    )(*args)


def owner_mix(codes, adj, owners):
    return pl.pallas_call(
        owners_kernel,
        grid_spec=pltpu.PrefetchScalarGridSpec(
            num_scalar_prefetch=1, grid=(1,), in_specs=[whole(adj.shape), whole(owners.shape)],
            out_specs=whole((GB * GB, BLK, C)), scratch_shapes=[pltpu.VMEM((EXT * EXT * BLK, C), bf16)]),
        out_shape=jax.ShapeDtypeStruct((GB * GB, BLK, C), bf16),
        compiler_params=PARAMS,
        name="owner_mix",
        cost_estimate=pl.CostEstimate(flops=GB * GB * NB * 2 * BLK * BLK * C, bytes_accessed=2 << 20, transcendentals=0),
    )(codes, adj, owners)


def shift(block, axis, up):
    count = lax.axis_size(axis)
    pairs = [(i, i + 1) for i in range(count - 1)]
    return lax.ppermute(block, axis, pairs if up else [(b, a) for a, b in pairs])


def corners(yl, yr):
    low, high = slice(0, BLK), slice((GB - 1) * BLK, GB * BLK)
    cu = shift(jnp.concatenate([yl[:, high], yr[:, high]], axis=1), "rx", True)
    cd = shift(jnp.concatenate([yl[:, low], yr[:, low]], axis=1), "rx", False)
    return cu, cd


def exchange(left, right, top, bottom):
    yl = shift(right, "ry", True)
    yr = shift(left, "ry", False)
    xu = shift(bottom, "rx", True)
    xd = shift(top, "rx", False)
    return (yl, yr, xu, xd) + corners(yl, yr)


def grown(own):
    own = own.reshape(GB, GB, BLK)
    wide = jnp.concatenate([shift(own[:, GB - 1 :], "ry", True), own, shift(own[:, :1], "ry", False)], axis=1)
    tall = jnp.concatenate([shift(wide[GB - 1 :], "rx", True), wide, shift(wide[:1], "rx", False)], axis=0)
    return jnp.pad(tall.reshape(EXT * EXT, BLK), ((0, 7), (0, 0)))


def on_device(noisy_input, adjacency, neighbours, norm_gain, w_mix, pool_weight, cluster, owner_ids, w_coarse, w_region, w_out):
    steps = noisy_input.shape[1]
    x = noisy_input.transpose(1, 0, 2)
    codes = neighbours.reshape(-1)
    crows = owner_ids.shape[0]
    devices = lax.axis_size("rx") * lax.axis_size("ry")
    squares = x.reshape(steps, GB, GB, BLK, C)

    firsts = [sum(CHUNKS[:i]) for i in range(len(CHUNKS))]
    halos = []
    for first, nt in zip(firsts, CHUNKS):
        part = squares[first : first + nt]
        flat = lambda v: v.reshape(nt, GB * BLK, C)
        halos.append(exchange(flat(part[:, :, 0]), flat(part[:, :, GB - 1]), flat(part[:, 0]), flat(part[:, GB - 1])))

    owner = owner_ids[:, 0]
    coarse = jnp.arange(crows, dtype=jnp.int32)
    ids = jnp.arange(devices, dtype=jnp.int32)
    hit = cluster[None, :] == coarse[:, None]
    pool = jnp.where(hit, pool_weight[None, :], jnp.zeros((), bf16))
    unpool = (cluster[:, None] == coarse[None, :]).astype(bf16)
    spread = (owner[None, :] == ids[:, None]).astype(bf16)
    node_owner = jnp.sum(jnp.where(hit, owner[:, None], 0), axis=0)
    hot = (node_owner[:, None] == ids[None, :]).astype(bf16)
    mown = owner_mix(codes, adjacency, grown((node_owner + 1).astype(bf16)))

    gain = norm_gain.reshape(1, C)
    results = []
    for i, (first, nt) in enumerate(zip(firsts, CHUNKS)):
        d1, dl, dr, du, dd, part = encode(codes, x, first, nt, *halos[i], adjacency, gain, w_mix, w_coarse, pool, unpool, spread)
        second = exchange(dl, dr, du, dd)
        arrived = lax.all_to_all(part, ("rx", "ry"), split_axis=0, concat_axis=0, tiled=True)
        region = (jnp.sum(arrived.astype(f32), axis=0, keepdims=True) / float(crows)).astype(bf16)
        everyone = jnp.broadcast_to(region, (devices, nt * C))
        region = lax.all_to_all(everyone, ("rx", "ry"), split_axis=0, concat_axis=0, tiled=True)
        results.append((d1, second, region))
    out = None
    for i, (first, nt) in enumerate(zip(firsts, CHUNKS)):
        d1, second, region = results[i]
        out = decode(codes, d1, first, nt, steps, *second, adjacency, mown, region, w_region, w_out, hot, out)
    return out.transpose(1, 0, 2)


def solution(mesh):
    nodes = P(("rx", "ry"))
    in_specs = (
        P(("rx", "ry"), None, None),
        P(("rx", "ry"), None, None, None),
        P(("rx", "ry"), None),
        P(),
        P(),
        nodes,
        nodes,
        P(("rx", "ry"), None),
        P(),
        P(),
        P(),
    )
    out_specs = P(("rx", "ry"), None, None)
    return jax.shard_map(on_device, mesh=mesh, in_specs=in_specs, out_specs=out_specs, check_vma=False)
```

```python
import functools
import jax
import jax.numpy as jnp
from jax import lax
from jax.experimental import pallas as pl
from jax.experimental.pallas import tpu as pltpu
from jax.sharding import PartitionSpec as P

GB, BLK, NB, C = 3, 128, 6, 128
EXT = GB + 2
ROWS = GB * GB * BLK
SIDE = GB * BLK
PAIR = 2
WIDE = PAIR * C
LATE = [(0, 3 + 3), (3, 3), (6, 0), (0, 0), (6, 6), (2, 3 + 5), (5, 5), (8, 2), (2, 2), (8, 8)]
bf16, f32 = jnp.bfloat16, jnp.float32


def silu(v):
    return v / (1.0 + jnp.exp(-v))


def dot(a, b):
    return jnp.dot(a, b, preferred_element_type=f32)


def span(k):
    return slice(k * BLK, (k + 1) * BLK)


def ext_row(codes, j, n):
    code = codes[j * NB + n]
    e = (j // GB + code // 3) * EXT + j % GB + code % 3
    return pl.ds(pl.multiple_of(e * BLK, BLK), BLK)


def fill(ext, own, yl, yr, xu, xd):
    @pl.when(pl.program_id(0) == 0)
    def _():
        for e in (0, EXT - 1, 2 * EXT, 3 * EXT - 1, (EXT - 1) * EXT, EXT * EXT - 1):
            ext[span(e), :] = jnp.zeros((BLK, WIDE), bf16)

    for s in range(PAIR):
        lanes = span(s)

        def put(row, col, block):
            ext[span(row * EXT + col), lanes] = block

        for a in range(GB):
            for b in range(GB):
                put(a + 1, b + 1, own[s, span(a * GB + b), :])
            put(0, a + 1, xu[s, span(a), :])
            put(EXT - 1, a + 1, xd[s, span(a), :])
        for e, row in enumerate((1, GB)):
            put(row, 0, yl[s, span(e), :])
            put(row, EXT - 1, yr[s, span(e), :])


def early_sum(codes, adj, ext, j):
    weights = jnp.concatenate([adj[j, n] for n in range(NB)], axis=1)
    feats = jnp.concatenate([ext[ext_row(codes, j, n), :] for n in range(NB)], axis=0)
    return dot(weights, feats)


def late_sum(late, j, mids, ups, downs):
    side = 0 if j % GB == 0 else 1
    k = side * 5 + j // GB
    if j // GB == 1:
        return dot(late[k], mids[side])
    corner, block = (3, ups[side]) if j // GB == 0 else (4, downs[side])
    return dot(jnp.concatenate([late[k], late[side * 5 + corner]], axis=1), jnp.concatenate([mids[side], block], axis=0))


def joined(ref, k):
    return jnp.concatenate([ref[s, span(k), :] for s in range(PAIR)], axis=1)


def mix_in(diffused, base, gain, w_mix):
    v = diffused.astype(bf16).astype(f32)
    ms = jnp.mean(v * v, axis=1, keepdims=True)
    normed = (v * lax.rsqrt(ms + 1e-6) * gain[...]).astype(bf16)
    return (base.astype(f32) + silu(dot(normed, w_mix[...]))).astype(bf16)


def encode_early(codes, own, yl, yr, xu, xd, adj, gain, w_mix, acc, mid, ext):
    fill(ext, own, yl, yr, xu, xd)
    for j in range(GB * GB):
        total = early_sum(codes, adj, ext, j)
        a, b = j // GB, j % GB
        for s in range(PAIR):
            v = total[:, span(s)]
            if b == 1:
                mid[s, span(a), :] = mix_in(v, own[s, span(j), :], gain, w_mix)
            else:
                acc[s, span(a if b == 0 else GB + a), :] = v


def encode_late(own, acc, mid, ml, mr, cu, cd, late, gain, w_mix, w_coarse, pool, unpool, spread, tails,
                d1, al, ar, bl, br, du, dd, part, enc):
    mids, ups, downs = (joined(ml, 0), joined(mr, 0)), (joined(cu, 0), joined(cu, 1)), (joined(cd, 0), joined(cd, 1))
    for j in range(GB * GB):
        a, b = j // GB, j % GB
        if b == 1:
            for s in range(PAIR):
                enc[span(j), span(s)] = mid[s, span(a), :]
            continue
        rest = late_sum(late, j, mids, ups, downs)
        for s in range(PAIR):
            v = acc[s, span(a if b == 0 else GB + a), :] + rest[:, span(s)]
            enc[span(j), span(s)] = mix_in(v, own[s, span(j), :], gain, w_mix)
    pooled = dot(pool[...], enc[...]).astype(bf16)
    lifted = jnp.concatenate([silu(dot(pooled[:, span(s)], w_coarse[...])).astype(bf16) for s in range(PAIR)], axis=1)
    part[...] = dot(spread[...], lifted).astype(bf16)
    refined = (pooled.astype(f32) + lifted.astype(f32)).astype(bf16)
    for j in range(GB * GB):
        a, b = j // GB, j % GB
        back = (enc[span(j), :].astype(f32) + dot(unpool[span(j), :], refined)).astype(bf16)
        for s in range(PAIR):
            v = back[:, span(s)]
            d1[s, span(j), :] = v
            if b != 1 and a != 1:
                (al if b == 0 else ar)[s, span(a // 2), :] = v
            if b != 1 and a == 1:
                (bl if b == 0 else br)[s, :BLK, :] = v
                (bl if b == 0 else br)[s, BLK:, :] = tails[b // 2]
            if a == 0:
                du[s, span(b), :] = v
            if a == GB - 1:
                dd[s, span(b), :] = v


def decode_early(codes, own, yl, yr, xu, xd, adj, acc, ext):
    fill(ext, own, yl, yr, xu, xd)
    for j in range(GB * GB):
        total = early_sum(codes, adj, ext, j)
        for s in range(PAIR):
            acc[s, span(j), :] = total[:, span(s)]


def decode_late(own, acc, ml, mr, cu, cd, late, mown, region, w_region, w_out, hot, out):
    mids, ups, downs = (joined(ml, 0), joined(mr, 0)), (joined(cu, 0), joined(cu, 1)), (joined(cd, 0), joined(cd, 1))
    reach = jnp.concatenate([dot(region[:, span(s)], w_region[...]).astype(bf16) for s in range(PAIR)], axis=1)
    for j in range(GB * GB):
        rest = dot(mown[j], reach)
        if j % GB != 1:
            rest += late_sum(late, j, mids, ups, downs)
        extra = dot(hot[span(j), :], reach)
        for s in range(PAIR):
            second = (acc[s, span(j), :] + rest[:, span(s)]).astype(bf16)
            dec = (own[s, span(j), :].astype(f32) + extra[:, span(s)]).astype(bf16).astype(f32)
            out[s, span(j), :] = (dec + silu(dot(second, w_out[...]))).astype(bf16)


def late_kernel(codes, adj, late):
    for k, (j, code) in enumerate(LATE):
        total = jnp.zeros((BLK, BLK), f32)
        for n in range(NB):
            total += jnp.where(codes[j * NB + n] == code, adj[j, n].astype(f32), 0.0)
        late[k] = total.astype(bf16)


def owners_kernel(codes, adj, owners, mown, hot):
    ids = lax.broadcasted_iota(jnp.int32, (C, BLK), 0)
    for e in range(EXT * EXT):
        a, b = e // EXT, e % EXT
        if b in (0, EXT - 1):
            k = 32 + (b > 0) * TAIL + a
        elif a in (0, EXT - 1):
            k = 16 + (a > 0) * TAIL + b - 1
        else:
            k = (a - 1) * GB + b - 1
        row = owners[k : k + 1, :].astype(f32).astype(jnp.int32) - 1
        hot[span(e), :] = (ids == row).astype(f32).astype(bf16)
    for j in range(GB * GB):
        acc = jnp.zeros((BLK, C), f32)
        for n in range(NB):
            acc += lax.dot_general(
                adj[j, n], hot[ext_row(codes, j, n), :], (((1,), (1,)), ((), ())), preferred_element_type=f32
            )
        mown[j] = acc.astype(bf16)


def whole(shape):
    return pl.BlockSpec(shape, lambda p, *_: (0,) * len(shape), pipeline_mode=pl.Buffered(1))


def by_step(rows):
    return pl.BlockSpec((PAIR, rows, C), lambda p, *_: (p, 0, 0))


def by_lane(rows):
    return pl.BlockSpec((rows, WIDE), lambda p, *_: (0, p))


def call(kernel, name, steps, args, specs, outs, out_specs, scratch, flops, prefetch=0, exps=0):
    size = lambda v: v.size * v.dtype.itemsize
    return pl.pallas_call(
        kernel,
        grid_spec=pltpu.PrefetchScalarGridSpec(
            num_scalar_prefetch=prefetch, grid=(steps // PAIR,), in_specs=specs, out_specs=out_specs, scratch_shapes=scratch
        ),
        out_shape=outs,
        compiler_params=pltpu.CompilerParams(vmem_limit_bytes=VMEM << 20, dimension_semantics=("arbitrary",)),
        name=name,
        cost_estimate=pl.CostEstimate(
            flops=flops, bytes_accessed=sum(map(size, args)) + sum(map(size, outs)), transcendentals=exps
        ),
    )(*args)


VMEM = 28
TAIL = 8


def sds(shape, dtype=bf16):
    return jax.ShapeDtypeStruct(shape, dtype)


def shift(block, axis, up):
    count = lax.axis_size(axis)
    pairs = [(i, i + 1) for i in range(count - 1)]
    return lax.ppermute(block, axis, pairs if up else [(b, a) for a, b in pairs])


def corners(yl, yr):
    cu = shift(jnp.concatenate([yl[:, BLK:], yr[:, BLK:]], axis=1), "rx", True)
    cd = shift(jnp.concatenate([yl[:, :BLK], yr[:, :BLK]], axis=1), "rx", False)
    return cu, cd


def with_owners(block, owners):
    rows = jnp.broadcast_to(jnp.pad(owners, ((0, TAIL - GB), (0, 0)))[None], (block.shape[0], TAIL, C))
    return jnp.concatenate([block, rows], axis=1)


def on_device(noisy_input, adjacency, neighbours, norm_gain, w_mix, pool_weight, cluster, owner_ids, w_coarse, w_region, w_out):
    steps = noisy_input.shape[1]
    x = noisy_input.transpose(1, 0, 2)
    codes = neighbours.reshape(-1)
    crows = owner_ids.shape[0]
    devices = lax.axis_size("rx") * lax.axis_size("ry")
    squares = x.reshape(steps, GB, GB, BLK, C)
    flat = lambda v: v.reshape(steps, -1, C)
    work = steps * ROWS * C * 2

    owner = owner_ids[:, 0]
    coarse = jnp.arange(crows, dtype=jnp.int32)
    ids = jnp.arange(devices, dtype=jnp.int32)
    hit = cluster[None, :] == coarse[:, None]
    node_owner = jnp.sum(jnp.where(hit, owner[:, None], 0), axis=0)
    owners = (node_owner + 1).astype(bf16).reshape(GB * GB, BLK)

    yl = shift(flat(squares[:, ::2, GB - 1]), "ry", True)
    yr = shift(flat(squares[:, ::2, 0]), "ry", False)
    xu = shift(with_owners(flat(squares[:, GB - 1]), owners[-GB:]), "rx", True)
    xd = shift(with_owners(flat(squares[:, 0]), owners[:GB]), "rx", False)
    ml = shift(flat(squares[:, 1, GB - 1]), "ry", True)
    right = flat(squares[:, 1, 0])
    right, xu = lax.optimization_barrier((right, xu))
    mr = shift(right, "ry", False)
    pool = jnp.where(hit, pool_weight[None, :], jnp.zeros((), bf16))
    unpool = (cluster[:, None] == coarse[None, :]).astype(bf16)
    spread = (owner[None, :] == ids[:, None]).astype(bf16)
    hot = (node_owner[:, None] == ids[None, :]).astype(bf16)
    column = lambda b: jnp.concatenate([xu[0, SIDE + b : SIDE + b + 1], owners[b::GB], xd[0, SIDE + b : SIDE + b + 1]])
    tails = jnp.pad(jnp.stack([column(0), column(GB - 1)]), ((0, 0), (0, TAIL - EXT), (0, 0)))
    tops = jnp.stack([xu[0, SIDE:], xd[0, SIDE:]])
    gain = norm_gain.reshape(1, C)
    ext = pltpu.VMEM((EXT * EXT * BLK, WIDE), bf16)
    square = (BLK, C)

    (late,) = call(late_kernel, "late_weights", PAIR, [codes, adjacency], [whole(adjacency.shape)],
                   [sds((len(LATE),) + square)], [whole((len(LATE),) + square)], [], 1 << 20, prefetch=1)
    cu, cd = corners(yl, yr)
    xu, xd, late, pool, unpool, spread, hot, tails, tops = lax.optimization_barrier((xu, xd, late, pool, unpool, spread, hot, tails, tops))
    early = lambda: [by_step(ROWS)] + [by_step(v.shape[1]) for v in (yl, yr, xu, xd)] + [whole(adjacency.shape)]
    acc, mid = call(
        encode_early, "encode_early", steps, [codes, x, yl, yr, xu, xd, adjacency, gain, w_mix],
        early() + [whole((1, C)), whole(square)],
        [sds((steps, 2 * SIDE, C), f32), sds((steps, SIDE, C))], [by_step(2 * SIDE), by_step(SIDE)], [ext],
        work * (NB * BLK + C // 3), prefetch=1, exps=work // 6)
    halo = lambda: [by_step(v.shape[1]) for v in (ml, mr, cu, cd)] + [whole(late.shape)]
    d1, al, ar, bl, br, du, dd, part = call(
        encode_late, "encode_late", steps,
        [x, acc, mid, ml, mr, cu, cd, late, gain, w_mix, w_coarse, pool, unpool, spread, tails],
        [by_step(ROWS), by_step(2 * SIDE), by_step(SIDE)] + halo()
        + [whole((1, C)), whole(square), whole(square), whole(pool.shape), whole(unpool.shape), whole(spread.shape), whole(tails.shape)],
        [sds((steps, r, C)) for r in (ROWS, 2 * BLK, 2 * BLK, BLK + TAIL, BLK + TAIL, SIDE, SIDE)] + [sds((devices, steps * C))],
        [by_step(r) for r in (ROWS, 2 * BLK, 2 * BLK, BLK + TAIL, BLK + TAIL, SIDE, SIDE)] + [by_lane(devices)],
        [pltpu.VMEM((ROWS, WIDE), bf16)], work * (C + 3 * crows), exps=work // 3)

    yl = shift(ar, "ry", True)
    yr = shift(al, "ry", False)
    xu = shift(dd, "rx", True)
    xd = shift(du, "rx", False)
    ml = shift(br, "ry", True)
    bl, xu = lax.optimization_barrier((bl, xu))
    mr = shift(bl, "ry", False)
    half = (devices, 2, steps * C // 2)
    arrived = lax.all_to_all(part.reshape(half), ("rx", "ry"), split_axis=0, concat_axis=0, tiled=True)
    region = (jnp.sum(arrived.astype(f32), axis=0, keepdims=True) / float(crows)).astype(bf16)
    region = lax.all_to_all(jnp.broadcast_to(region, half), ("rx", "ry"), split_axis=0, concat_axis=0, tiled=True)
    region = region.reshape(devices, steps * C)
    cu, cd = corners(yl, yr)
    owners = jnp.concatenate([owners, jnp.zeros((16 - GB * GB, BLK), bf16), tops[0], tops[1], ml[0, BLK:], mr[0, BLK:]])
    (mown,) = call(owners_kernel, "owner_mix", PAIR, [codes, adjacency, owners], [whole(adjacency.shape), whole(owners.shape)],
                   [sds((GB * GB,) + square)], [whole((GB * GB,) + square)],
                   [pltpu.VMEM((EXT * EXT * BLK, C), bf16)], GB * GB * NB * 2 * BLK**3, prefetch=1)
    (acc,) = call(decode_early, "decode_early", steps, [codes, d1, yl, yr, xu, xd, adjacency], early(),
                  [sds((steps, ROWS, C), f32)], [by_step(ROWS)], [ext], work * NB * BLK, prefetch=1)
    (out,) = call(
        decode_late, "decode_late", steps, [d1, acc, ml, mr, cu, cd, late, mown, region, w_region, w_out, hot],
        [by_step(ROWS)] * 2 + halo()
        + [whole(mown.shape), by_lane(devices), whole(square), whole(square), whole(hot.shape)],
        [sds((steps, ROWS, C))], [by_step(ROWS)], [], work * 3 * C, exps=work // 2)
    return out.transpose(1, 0, 2)


def solution(mesh):
    nodes = P(("rx", "ry"))
    in_specs = (
        P(("rx", "ry"), None, None),
        P(("rx", "ry"), None, None, None),
        P(("rx", "ry"), None),
        P(),
        P(),
        nodes,
        nodes,
        P(("rx", "ry"), None),
        P(),
        P(),
        P(),
    )
    out_specs = P(("rx", "ry"), None, None)
    return jax.shard_map(on_device, mesh=mesh, in_specs=in_specs, out_specs=out_specs, check_vma=False)
```

```python
import functools
import jax
import jax.numpy as jnp
from jax import lax
from jax.experimental import pallas as pl
from jax.experimental.pallas import tpu as pltpu
from jax.sharding import PartitionSpec as P

GB, BLK, NB, C = 3, 128, 6, 128
EXT = GB + 2
ROWS = GB * GB * BLK
SIDE = GB * BLK
PAIR = 2
WIDE = PAIR * C
bf16, f32 = jnp.bfloat16, jnp.float32


def silu(v):
    return v / (1.0 + jnp.exp(-v))


def dot(a, b):
    return jnp.dot(a, b, preferred_element_type=f32)


def span(k):
    return slice(k * BLK, (k + 1) * BLK)


def ext_row(codes, j, n):
    code = codes[j * NB + n]
    e = (j // GB + code // 3) * EXT + j % GB + code % 3
    return pl.ds(pl.multiple_of(e * BLK, BLK), BLK)


def fill(ext, own, xu=None, xd=None):
    @pl.when(pl.program_id(0) == 0)
    def _():
        if xu is None:
            ext[...] = jnp.zeros(ext.shape, bf16)
        for e in range(EXT):
            ext[span(e * EXT), :] = jnp.zeros((BLK, WIDE), bf16)
            ext[span(e * EXT + EXT - 1), :] = jnp.zeros((BLK, WIDE), bf16)

    for s in range(PAIR):
        lanes = span(s)

        def put(row, col, block):
            ext[span(row * EXT + col), lanes] = block

        for a in range(GB):
            for b in range(GB):
                put(a + 1, b + 1, own[s, span(a * GB + b), :])
            if xu is not None:
                put(0, a + 1, xu[s, span(a), :])
                put(EXT - 1, a + 1, xd[s, span(a), :])


def early_sum(codes, adj, ext, j):
    weights = jnp.concatenate([adj[j, n] for n in range(NB)], axis=1)
    feats = jnp.concatenate([ext[ext_row(codes, j, n), :] for n in range(NB)], axis=0)
    return dot(weights, feats)


def side_term(late, j, columns):
    a, side = j // GB, int(j % GB > 0)
    return late[side * GB + a], columns[side][a * BLK : (a + GB) * BLK, :]


def row_term(late, j, rows):
    b, low = j % GB, int(j >= GB)
    first, last = max(b - 1, 0), min(b + 1, GB - 1)
    lanes = slice((first - b + 1) * BLK, (last - b + 2) * BLK)
    return late[(2 + low) * GB + b][:, lanes], rows[low][first * BLK : (last + 1) * BLK, :]


def side_columns(yl, yr, cu, cd):
    return [jnp.concatenate([joined(cu, k)] + [joined(y, a) for a in range(GB)] + [joined(cd, k)], axis=0)
            for k, y in enumerate((yl, yr))]


def joined(ref, k):
    return jnp.concatenate([ref[s, span(k), :] for s in range(PAIR)], axis=1)


def mix_in(diffused, base, gain, w_mix):
    v = diffused.astype(bf16).astype(f32)
    ms = jnp.mean(v * v, axis=1, keepdims=True)
    normed = (v * lax.rsqrt(ms + 1e-6) * gain[...]).astype(bf16)
    return (base.astype(f32) + silu(dot(normed, w_mix[...]))).astype(bf16)


def encode_early(codes, own, xu, xd, adj, gain, w_mix, acc, mid, ext):
    fill(ext, own, xu, xd)
    for j in range(GB * GB):
        total = early_sum(codes, adj, ext, j)
        a, b = j // GB, j % GB
        for s in range(PAIR):
            v = total[:, span(s)]
            if b == 1:
                mid[s, span(a), :] = mix_in(v, own[s, span(j), :], gain, w_mix)
            else:
                acc[s, span(a if b == 0 else GB + a), :] = v


def encode_late(own, acc, mid, yl, yr, cu, cd, cut, cdt, late, gain, w_mix, w_coarse, pool, unpool, spread, owners,
                d1, dl, dr, part, enc):
    columns = side_columns(yl, yr, cu, cd)
    for j in range(GB * GB):
        a, b = j // GB, j % GB
        if b == 1:
            for s in range(PAIR):
                enc[span(j), span(s)] = mid[s, span(a), :]
            continue
        rest = dot(*side_term(late, j, columns))
        for s in range(PAIR):
            v = acc[s, span(a if b == 0 else GB + a), :] + rest[:, span(s)]
            enc[span(j), span(s)] = mix_in(v, own[s, span(j), :], gain, w_mix)
    pooled = dot(pool[...], enc[...]).astype(bf16)
    lifted = jnp.concatenate([silu(dot(pooled[:, span(s)], w_coarse[...])).astype(bf16) for s in range(PAIR)], axis=1)
    part[...] = dot(spread[...], lifted).astype(bf16)
    refined = (pooled.astype(f32) + lifted.astype(f32)).astype(bf16)
    for s in range(PAIR):
        for k, out in ((0, dl), (GB - 1, dr)):
            ids = [cut[0, k : k + 1, :]] + [owners[a * GB + k : a * GB + k + 1, :] for a in range(GB)]
            ids += [cdt[0, k : k + 1, :], jnp.zeros((TAIL - EXT, C), bf16)]
            out[s, SIDE:, :] = jnp.concatenate([v.astype(f32) for v in ids], axis=0).astype(bf16)
    for j in range(GB * GB):
        a, b = j // GB, j % GB
        back = (enc[span(j), :].astype(f32) + dot(unpool[span(j), :], refined)).astype(bf16)
        for s in range(PAIR):
            v = back[:, span(s)]
            d1[s, span(j), :] = v
            if b != 1:
                (dl if b == 0 else dr)[s, span(a), :] = v


def decode_early(codes, own, adj, acc, ext):
    fill(ext, own)
    for j in range(GB * GB):
        total = early_sum(codes, adj, ext, j)
        for s in range(PAIR):
            acc[s, span(j), :] = total[:, span(s)]


def decode_late(own, acc, yl, yr, cu, cd, xu, xd, late, mown, region, w_region, w_out, hot, out):
    columns = side_columns(yl, yr, cu, cd)
    rows = [jnp.concatenate([joined(x, b) for b in range(GB)], axis=0) for x in (xu, xd)]
    reach = jnp.concatenate([dot(region[:, span(s)], w_region[...]).astype(bf16) for s in range(PAIR)], axis=1)
    for j in range(GB * GB):
        terms = [(mown[j], reach)]
        if j % GB != 1:
            terms.append(side_term(late, j, columns))
        if j // GB != 1:
            terms.append(row_term(late, j, rows))
        rest = dot(jnp.concatenate([w for w, _ in terms], axis=1), jnp.concatenate([v for _, v in terms], axis=0))
        extra = dot(hot[span(j), :], reach)
        for s in range(PAIR):
            second = (acc[s, span(j), :] + rest[:, span(s)]).astype(bf16)
            dec = (own[s, span(j), :].astype(f32) + extra[:, span(s)]).astype(bf16).astype(f32)
            out[s, span(j), :] = (dec + silu(dot(second, w_out[...]))).astype(bf16)


def late_kernel(codes, adj, late):
    for k in range(4 * GB):
        side, a = k // GB % 2, k % GB
        j = a * GB + side * (GB - 1) if k < 2 * GB else side * (GB - 1) * GB + a
        for d in range(GB):
            code = d * GB + side * (GB - 1) if k < 2 * GB else side * (GB - 1) * GB + d
            total = jnp.zeros((BLK, BLK), f32)
            for n in range(NB):
                total += jnp.where(codes[j * NB + n] == code, adj[j, n].astype(f32), 0.0)
            late[k, :, span(d)] = total.astype(bf16)


def owners_kernel(codes, adj, owners, cut, cdt, ylt, yrt, mown, hot):
    ids = lax.broadcasted_iota(jnp.int32, (C, BLK), 0)
    for e in range(EXT * EXT):
        a, b = e // EXT, e % EXT
        if b in (0, EXT - 1):
            row = (yrt if b else ylt)[0, a : a + 1, :]
        elif a in (0, EXT - 1):
            row = (cdt if a else cut)[0, b - 1 : b, :]
        else:
            k = (a - 1) * GB + b - 1
            row = owners[k : k + 1, :]
        row = row.astype(f32).astype(jnp.int32) - 1
        hot[span(e), :] = (ids == row).astype(f32).astype(bf16)
    for j in range(GB * GB):
        acc = jnp.zeros((BLK, C), f32)
        for n in range(NB):
            acc += lax.dot_general(
                adj[j, n], hot[ext_row(codes, j, n), :], (((1,), (1,)), ((), ())), preferred_element_type=f32
            )
        mown[j] = acc.astype(bf16)


def whole(shape):
    return pl.BlockSpec(shape, lambda p, *_: (0,) * len(shape), pipeline_mode=pl.Buffered(1))


def by_step(rows):
    return pl.BlockSpec((PAIR, rows, C), lambda p, *_: (p, 0, 0))


def by_lane(rows):
    return pl.BlockSpec((rows, WIDE), lambda p, *_: (0, p))


def call(kernel, name, steps, args, specs, outs, out_specs, scratch, flops, prefetch=0, exps=0, vmem=60):
    size = lambda v: v.size * v.dtype.itemsize
    return pl.pallas_call(
        kernel,
        grid_spec=pltpu.PrefetchScalarGridSpec(
            num_scalar_prefetch=prefetch, grid=(steps // PAIR,), in_specs=specs, out_specs=out_specs, scratch_shapes=scratch
        ),
        out_shape=outs,
        compiler_params=pltpu.CompilerParams(vmem_limit_bytes=vmem << 20, dimension_semantics=("arbitrary",)),
        name=name,
        cost_estimate=pl.CostEstimate(
            flops=flops, bytes_accessed=sum(map(size, args)) + sum(map(size, outs)), transcendentals=exps
        ),
    )(*args)


TAIL = 8
HINT = 1 << 34


def sds(shape, dtype=bf16):
    return jax.ShapeDtypeStruct(shape, dtype)


def shift(block, axis, up):
    count = lax.axis_size(axis)
    pairs = [(i, i + 1) for i in range(count - 1)]
    return lax.ppermute(block, axis, pairs if up else [(b, a) for a, b in pairs])


def copy_all(copies):
    for copy in copies:
        copy.start()
    for copy in copies:
        copy.wait()


def corner_kernel(yl, yr, tails, up, down, sems):
    copies = []
    for e, (out, row) in enumerate(((up, GB - 1), (down, 0))):
        for k, y in enumerate((yl, yr)):
            copies.append(pltpu.make_async_copy(y.at[:, span(row), :], out.at[:, span(k), :], sems.at[3 * e + k]))
        copies.append(pltpu.make_async_copy(tails.at[e], out.at[0, 2 * BLK :, :], sems.at[3 * e + 2]))
    copy_all(copies)


def rows_kernel(x, top, bottom, sems):
    copy_all([
        pltpu.make_async_copy(x.at[:, span(0).start : SIDE, :], top, sems.at[0]),
        pltpu.make_async_copy(x.at[:, ROWS - SIDE :, :], bottom, sems.at[1]),
    ])


def place(n):
    return [pl.BlockSpec(memory_space=pl.ANY)] * n


def rows_halo(x):
    top, bottom = call(rows_kernel, "pack_rows", PAIR, [x], place(1), [sds((x.shape[0], SIDE, C))] * 2, place(2),
                       [pltpu.SemaphoreType.DMA((2,))], HINT)
    return shift(bottom, "rx", True), shift(top, "rx", False), top


def corners(yl, yr, tails):
    shape = sds((yl.shape[0], 2 * BLK + TAIL, C))
    up, down = call(corner_kernel, "pack_corners", PAIR, [yl, yr, tails], place(3), [shape] * 2, place(2),
                    [pltpu.SemaphoreType.DMA((6,))], 1, vmem=4)
    return shift(up, "rx", True), shift(down, "rx", False)


def on_device(noisy_input, adjacency, neighbours, norm_gain, w_mix, pool_weight, cluster, owner_ids, w_coarse, w_region, w_out):
    steps = noisy_input.shape[1]
    x = noisy_input.transpose(1, 0, 2)
    codes = neighbours.reshape(-1)
    crows = owner_ids.shape[0]
    devices = lax.axis_size("rx") * lax.axis_size("ry")
    squares = x.reshape(steps, GB, GB, BLK, C)
    flat = lambda v: v.reshape(steps, -1, C)
    work = steps * ROWS * C * 2

    owner = owner_ids[:, 0]
    coarse = jnp.arange(crows, dtype=jnp.int32)
    ids = jnp.arange(devices, dtype=jnp.int32)
    hit = cluster[None, :] == coarse[:, None]
    node_owner = jnp.sum(jnp.where(hit, owner[:, None], 0), axis=0)
    owners = (node_owner + 1).astype(bf16).reshape(GB * GB, BLK)

    right, left = flat(squares[:, :, GB - 1]), flat(squares[:, :, 0])
    yl = shift(right, "ry", True)
    yr = shift(left, "ry", False)
    x_late, _, _ = lax.optimization_barrier((x, right, left))
    xu, xd, _ = rows_halo(x_late)
    pool = jnp.where(hit, pool_weight[None, :], jnp.zeros((), bf16))
    unpool = (cluster[:, None] == coarse[None, :]).astype(bf16)
    spread = (owner[None, :] == ids[:, None]).astype(bf16)
    hot = (node_owner[:, None] == ids[None, :]).astype(bf16)
    triple = lambda a: jnp.pad(owners[a * GB : (a + 1) * GB], ((0, TAIL - GB), (0, 0)))
    tails = jnp.stack([triple(GB - 1), triple(0)])
    owners = jnp.pad(owners, ((0, 16 - GB * GB), (0, 0)))
    gain = norm_gain.reshape(1, C)
    ext = pltpu.VMEM((EXT * EXT * BLK, WIDE), bf16)
    square = (BLK, C)

    (late,) = call(late_kernel, "late_weights", PAIR, [codes, adjacency], [whole(adjacency.shape)],
                   [sds((4 * GB, BLK, SIDE))], [whole((4 * GB, BLK, SIDE))], [], 1 << 20, prefetch=1)
    xu, xd, late, pool, unpool, spread, hot, tails, owners = lax.optimization_barrier((xu, xd, late, pool, unpool, spread, hot, tails, owners))
    early = lambda: [by_step(ROWS)] + [by_step(v.shape[1]) for v in (xu, xd)] + [whole(adjacency.shape)]
    acc, mid = call(
        encode_early, "encode_early", steps, [codes, x, xu, xd, adjacency, gain, w_mix],
        early() + [whole((1, C)), whole(square)],
        [sds((steps, 2 * SIDE, C), f32), sds((steps, SIDE, C))], [by_step(2 * SIDE), by_step(SIDE)], [ext],
        work * (NB * BLK + C // 3), prefetch=1, exps=work // 6)
    yl, yr, acc, mid = lax.optimization_barrier((yl, yr, acc, mid))
    cu, cd = corners(yl, yr, tails)
    halo = lambda: [by_step(v.shape[1]) for v in (yl, yr, cu, cd)]
    tail = lambda v: pl.BlockSpec((1, TAIL, C), lambda p, *_: (0, v.shape[1] // TAIL - 1, 0))
    first_cu, first_cd = cu, cd
    d1, dl, dr, part = call(
        encode_late, "encode_late", steps,
        [x, acc, mid, yl, yr, cu, cd, cu, cd, late, gain, w_mix, w_coarse, pool, unpool, spread, owners],
        [by_step(ROWS), by_step(2 * SIDE), by_step(SIDE)] + halo() + [tail(cu), tail(cd), whole(late.shape)]
        + [whole((1, C)), whole(square), whole(square), whole(pool.shape), whole(unpool.shape), whole(spread.shape), whole(owners.shape)],
        [sds((steps, r, C)) for r in (ROWS, SIDE + TAIL, SIDE + TAIL)] + [sds((devices, steps * C))],
        [by_step(r) for r in (ROWS, SIDE + TAIL, SIDE + TAIL)] + [by_lane(devices)],
        [pltpu.VMEM((ROWS, WIDE), bf16)], work * (C + 3 * crows), exps=work // 3)

    yl = shift(dr, "ry", True)
    yr = shift(dl, "ry", False)
    xu, xd, top = rows_halo(d1)
    part, _ = lax.optimization_barrier((part, top))
    (acc,) = call(decode_early, "decode_early", steps, [codes, d1, adjacency], [by_step(ROWS), whole(adjacency.shape)],
                  [sds((steps, ROWS, C), f32)], [by_step(ROWS)], [ext], work * NB * BLK, prefetch=1)
    half = (devices, 2, steps * C // 2)
    arrived = lax.all_to_all(part.reshape(half), ("rx", "ry"), split_axis=0, concat_axis=0, tiled=True)
    region = (jnp.sum(arrived.astype(f32), axis=0, keepdims=True) / float(crows)).astype(bf16)
    everyone = jnp.broadcast_to(region, half)
    everyone, _, _, _ = lax.optimization_barrier((everyone, xu, xd, acc))
    region = lax.all_to_all(everyone, ("rx", "ry"), split_axis=0, concat_axis=0, tiled=True)
    region = region.reshape(devices, steps * C)
    yl, yr, _, _ = lax.optimization_barrier((yl, yr, acc, everyone))
    cu, cd = corners(yl, yr, tails)
    (mown,) = call(owners_kernel, "owner_mix", PAIR, [codes, adjacency, owners, first_cu, first_cd, yl, yr],
                   [whole(adjacency.shape), whole(owners.shape)] + [tail(v) for v in (first_cu, first_cd, yl, yr)],
                   [sds((GB * GB,) + square)], [whole((GB * GB,) + square)],
                   [pltpu.VMEM((EXT * EXT * BLK, C), bf16)], HINT, prefetch=1)
    (out,) = call(
        decode_late, "decode_late", steps, [d1, acc, yl, yr, cu, cd, xu, xd, late, mown, region, w_region, w_out, hot],
        [by_step(ROWS)] * 2 + halo() + [by_step(SIDE)] * 2 + [whole(late.shape)]
        + [whole(mown.shape), by_lane(devices), whole(square), whole(square), whole(hot.shape)],
        [sds((steps, ROWS, C))], [by_step(ROWS)], [], work * 3 * C, exps=work // 2)
    return out.transpose(1, 0, 2)


def solution(mesh):
    nodes = P(("rx", "ry"))
    in_specs = (
        P(("rx", "ry"), None, None),
        P(("rx", "ry"), None, None, None),
        P(("rx", "ry"), None),
        P(),
        P(),
        nodes,
        nodes,
        P(("rx", "ry"), None),
        P(),
        P(),
        P(),
    )
    out_specs = P(("rx", "ry"), None, None)
    return jax.shard_map(on_device, mesh=mesh, in_specs=in_specs, out_specs=out_specs, check_vma=False)
```

```python
import functools
import jax
import jax.numpy as jnp
from jax import lax
from jax.experimental import pallas as pl
from jax.experimental.pallas import tpu as pltpu
from jax.sharding import PartitionSpec as P

GB, BLK, NB, C = 3, 128, 6, 128
EXT = GB + 2
ROWS = GB * GB * BLK
SIDE = GB * BLK
PAIR = 4
WIDE = PAIR * C
bf16, f32 = jnp.bfloat16, jnp.float32
ACC = bf16


def silu(v):
    return v / (1.0 + jnp.exp(-v))


def dot(a, b):
    return jnp.dot(a, b, preferred_element_type=f32)


def span(k):
    return slice(k * BLK, (k + 1) * BLK)


def ext_row(codes, j, n):
    code = codes[j * NB + n]
    e = (j // GB + code // 3) * EXT + j % GB + code % 3
    return pl.ds(pl.multiple_of(e * BLK, BLK), BLK)


def fill(ext, own, xu=None, xd=None):
    @pl.when(pl.program_id(0) == 0)
    def _():
        if xu is None:
            ext[...] = jnp.zeros(ext.shape, bf16)
        for e in range(EXT):
            ext[span(e * EXT), :] = jnp.zeros((BLK, WIDE), bf16)
            ext[span(e * EXT + EXT - 1), :] = jnp.zeros((BLK, WIDE), bf16)

    for s in range(PAIR):
        lanes = span(s)

        def put(row, col, block):
            ext[span(row * EXT + col), lanes] = block

        for a in range(GB):
            for b in range(GB):
                put(a + 1, b + 1, own[s, span(a * GB + b), :])
            if xu is not None:
                put(0, a + 1, xu[s, span(a), :])
                put(EXT - 1, a + 1, xd[s, span(a), :])


def early_sum(codes, adj, ext, j):
    weights = jnp.concatenate([adj[j, n] for n in range(NB)], axis=1)
    feats = jnp.concatenate([ext[ext_row(codes, j, n), :] for n in range(NB)], axis=0)
    return dot(weights, feats)


def side_term(late, j, columns):
    a, side = j // GB, int(j % GB > 0)
    return late[side * GB + a], columns[side][a * BLK : (a + GB) * BLK, :]


def row_term(late, j, rows):
    b, low = j % GB, int(j >= GB)
    first, last = max(b - 1, 0), min(b + 1, GB - 1)
    lanes = slice((first - b + 1) * BLK, (last - b + 2) * BLK)
    return late[(2 + low) * GB + b][:, lanes], rows[low][first * BLK : (last + 1) * BLK, :]


def side_columns(yl, yr, cu, cd):
    return [jnp.concatenate([joined(cu, k)] + [joined(y, a) for a in range(GB)] + [joined(cd, k)], axis=0)
            for k, y in enumerate((yl, yr))]


def joined(ref, k):
    return jnp.concatenate([ref[s, span(k), :] for s in range(PAIR)], axis=1)


def twice(w):
    zero = jnp.zeros((C, C), bf16)
    return jnp.concatenate([jnp.concatenate([w, zero], axis=1), jnp.concatenate([zero, w], axis=1)], axis=0)


def mix(values, w):
    parts = [dot(jnp.concatenate(values[s : s + 2], axis=1), w[...]) for s in range(0, PAIR, 2)]
    return [silu(parts[s // 2][:, span(s % 2)]) for s in range(PAIR)]


def norm(diffused, gain):
    v = diffused.astype(bf16).astype(f32)
    ms = jnp.mean(v * v, axis=1, keepdims=True)
    return (v * lax.rsqrt(ms + 1e-6) * gain[...]).astype(bf16)


def mix_in(diffused, own, j, gain, w_mix):
    mixed = mix([norm(v, gain) for v in diffused], w_mix)
    return [(own[s, span(j), :].astype(f32) + mixed[s]).astype(bf16) for s in range(PAIR)]


def encode_early(codes, own, xu, xd, adj, gain, w_mix, acc, mid, ext):
    fill(ext, own, xu, xd)
    for j in range(GB * GB):
        total = early_sum(codes, adj, ext, j)
        a, b = j // GB, j % GB
        parts = [total[:, span(s)] for s in range(PAIR)]
        if b == 1:
            parts = mix_in(parts, own, j, gain, w_mix)
        for s in range(PAIR):
            if b == 1:
                mid[s, span(a), :] = parts[s]
            else:
                acc[s, span(a if b == 0 else GB + a), :] = parts[s].astype(ACC)


def encode_late(own, acc, mid, yl, yr, cu, cd, cut, cdt, late, gain, w_mix, w_coarse, pool, unpool, spread, owners,
                d1, dl, dr, part, enc):
    columns = side_columns(yl, yr, cu, cd)
    for j in range(GB * GB):
        a, b = j // GB, j % GB
        if b == 1:
            for s in range(PAIR):
                enc[span(j), span(s)] = mid[s, span(a), :]
            continue
        rest = dot(*side_term(late, j, columns))
        parts = [acc[s, span(a if b == 0 else GB + a), :] + rest[:, span(s)] for s in range(PAIR)]
        for s, v in enumerate(mix_in(parts, own, j, gain, w_mix)):
            enc[span(j), span(s)] = v
    pooled = dot(pool[...], enc[...]).astype(bf16)
    lifted = jnp.concatenate(mix([pooled[:, span(s)] for s in range(PAIR)], w_coarse), axis=1).astype(bf16)
    part[...] = dot(spread[...], lifted).astype(bf16)
    refined = (pooled.astype(f32) + lifted.astype(f32)).astype(bf16)
    for s in range(PAIR):
        for k, out in ((0, dl), (GB - 1, dr)):
            ids = [cut[0, k : k + 1, :]] + [owners[a * GB + k : a * GB + k + 1, :] for a in range(GB)]
            ids += [cdt[0, k : k + 1, :], jnp.zeros((TAIL - EXT, C), bf16)]
            out[s, SIDE:, :] = jnp.concatenate([v.astype(f32) for v in ids], axis=0).astype(bf16)
    for j in range(GB * GB):
        a, b = j // GB, j % GB
        back = (enc[span(j), :].astype(f32) + dot(unpool[span(j), :], refined)).astype(bf16)
        for s in range(PAIR):
            v = back[:, span(s)]
            d1[s, span(j), :] = v
            if b != 1:
                (dl if b == 0 else dr)[s, span(a), :] = v


def decode_early(codes, own, adj, acc, ext):
    fill(ext, own)
    for j in range(GB * GB):
        total = early_sum(codes, adj, ext, j)
        for s in range(PAIR):
            acc[s, span(j), :] = total[:, span(s)].astype(ACC)


def decode_late(own, acc, yl, yr, cu, cd, xu, xd, late, mown, region, w_region, w_out, hot, out):
    columns = side_columns(yl, yr, cu, cd)
    rows = [jnp.concatenate([joined(x, b) for b in range(GB)], axis=0) for x in (xu, xd)]
    reach = jnp.concatenate([dot(region[:, span(s)], w_region[...]).astype(bf16) for s in range(PAIR)], axis=1)
    for j in range(GB * GB):
        terms = [(mown[j], reach)]
        if j % GB != 1:
            terms.append(side_term(late, j, columns))
        if j // GB != 1:
            terms.append(row_term(late, j, rows))
        rest = dot(jnp.concatenate([w for w, _ in terms], axis=1), jnp.concatenate([v for _, v in terms], axis=0))
        extra = dot(hot[span(j), :], reach)
        mixed = mix([(acc[s, span(j), :] + rest[:, span(s)]).astype(bf16) for s in range(PAIR)], w_out)
        for s in range(PAIR):
            dec = (own[s, span(j), :].astype(f32) + extra[:, span(s)]).astype(bf16).astype(f32)
            out[s, span(j), :] = (dec + mixed[s]).astype(bf16)


def late_kernel(codes, adj, late):
    for k in range(4 * GB):
        side, a = k // GB % 2, k % GB
        j = a * GB + side * (GB - 1) if k < 2 * GB else side * (GB - 1) * GB + a
        for d in range(GB):
            code = d * GB + side * (GB - 1) if k < 2 * GB else side * (GB - 1) * GB + d
            total = jnp.zeros((BLK, BLK), f32)
            for n in range(NB):
                total += jnp.where(codes[j * NB + n] == code, adj[j, n].astype(f32), 0.0)
            late[k, :, span(d)] = total.astype(bf16)


def owners_kernel(codes, adj, owners, cut, cdt, ylt, yrt, mown, hot):
    ids = lax.broadcasted_iota(jnp.int32, (C, BLK), 0)
    for e in range(EXT * EXT):
        a, b = e // EXT, e % EXT
        if b in (0, EXT - 1):
            row = (yrt if b else ylt)[0, a : a + 1, :]
        elif a in (0, EXT - 1):
            row = (cdt if a else cut)[0, b - 1 : b, :]
        else:
            k = (a - 1) * GB + b - 1
            row = owners[k : k + 1, :]
        row = row.astype(f32).astype(jnp.int32) - 1
        hot[span(e), :] = (ids == row).astype(f32).astype(bf16)
    for j in range(GB * GB):
        acc = jnp.zeros((BLK, C), f32)
        for n in range(NB):
            acc += lax.dot_general(
                adj[j, n], hot[ext_row(codes, j, n), :], (((1,), (1,)), ((), ())), preferred_element_type=f32
            )
        mown[j] = acc.astype(bf16)


def whole(shape):
    return pl.BlockSpec(shape, lambda p, *_: (0,) * len(shape), pipeline_mode=pl.Buffered(1))


def by_step(rows):
    return pl.BlockSpec((PAIR, rows, C), lambda p, *_: (p, 0, 0))


def by_lane(rows):
    return pl.BlockSpec((rows, WIDE), lambda p, *_: (0, p))


def call(kernel, name, steps, args, specs, outs, out_specs, scratch, flops, prefetch=0, exps=0, vmem=None):
    size = lambda v: v.size * v.dtype.itemsize
    return pl.pallas_call(
        kernel,
        grid_spec=pltpu.PrefetchScalarGridSpec(
            num_scalar_prefetch=prefetch, grid=(steps // PAIR,), in_specs=specs, out_specs=out_specs, scratch_shapes=scratch
        ),
        out_shape=outs,
        compiler_params=pltpu.CompilerParams(vmem_limit_bytes=(vmem or VMEM) << 20, dimension_semantics=("arbitrary",)),
        name=name,
        cost_estimate=pl.CostEstimate(
            flops=flops, bytes_accessed=sum(map(size, args)) + sum(map(size, outs)), transcendentals=exps
        ),
    )(*args)


TAIL = 8
HINT = 1 << 34
VMEM = 28


def sds(shape, dtype=bf16):
    return jax.ShapeDtypeStruct(shape, dtype)


def shift(block, axis, up):
    count = lax.axis_size(axis)
    pairs = [(i, i + 1) for i in range(count - 1)]
    return lax.ppermute(block, axis, pairs if up else [(b, a) for a, b in pairs])


def corner_kernel(lt, lb, rt, rb, tails, up, down):
    for out, left, right, k in ((up, lb, rb, 0), (down, lt, rt, 1)):
        out[:, :BLK, :] = left[...]
        out[:, BLK : 2 * BLK, :] = right[...]
        out[:, 2 * BLK :, :] = jnp.broadcast_to(tails[k][None], (out.shape[0], TAIL, C))


def rows_kernel(x, top, bottom):
    top[...] = x[:, :SIDE, :]
    bottom[...] = x[:, ROWS - SIDE :, :]


def rows_halo(x, hint):
    top, bottom = call(rows_kernel, "pack_rows", x.shape[0], [x], [by_step(ROWS)],
                       [sds((x.shape[0], SIDE, C))] * 2, [by_step(SIDE)] * 2, [], hint)
    return shift(bottom, "rx", True), shift(top, "rx", False), top


def corners(yl, yr, tails):
    steps = yl.shape[0]
    block = lambda a: pl.BlockSpec((PAIR, BLK, C), lambda p, *_: (p, a, 0))
    up, down = call(corner_kernel, "pack_corners", steps, [yl, yl, yr, yr, tails],
                    [block(0), block(GB - 1)] * 2 + [whole(tails.shape)],
                    [sds((steps, 2 * BLK + TAIL, C))] * 2, [by_step(2 * BLK + TAIL)] * 2, [], 1, vmem=8)
    return shift(up, "rx", True), shift(down, "rx", False)


def part_kernel(part, out):
    out[...] = part[...]


def on_device(noisy_input, adjacency, neighbours, norm_gain, w_mix, pool_weight, cluster, owner_ids, w_coarse, w_region, w_out):
    steps = noisy_input.shape[1]
    x = noisy_input.transpose(1, 0, 2)
    codes = neighbours.reshape(-1)
    crows = owner_ids.shape[0]
    devices = lax.axis_size("rx") * lax.axis_size("ry")
    squares = x.reshape(steps, GB, GB, BLK, C)
    flat = lambda v: v.reshape(steps, -1, C)
    work = steps * ROWS * C * 2

    owner = owner_ids[:, 0]
    coarse = jnp.arange(crows, dtype=jnp.int32)
    ids = jnp.arange(devices, dtype=jnp.int32)
    hit = cluster[None, :] == coarse[:, None]
    node_owner = jnp.sum(jnp.where(hit, owner[:, None], 0), axis=0)
    owners = (node_owner + 1).astype(bf16).reshape(GB * GB, BLK)

    right, left = flat(squares[:, :, GB - 1]), flat(squares[:, :, 0])
    yl = shift(right, "ry", True)
    yr = shift(left, "ry", False)
    x_late, _, _ = lax.optimization_barrier((x, right, left))
    xu, xd, _ = rows_halo(x_late, HINT)
    pool = jnp.where(hit, pool_weight[None, :], jnp.zeros((), bf16))
    unpool = (cluster[:, None] == coarse[None, :]).astype(bf16)
    spread = (owner[None, :] == ids[:, None]).astype(bf16)
    hot = (node_owner[:, None] == ids[None, :]).astype(bf16)
    triple = lambda a: jnp.pad(owners[a * GB : (a + 1) * GB], ((0, TAIL - GB), (0, 0)))
    tails = jnp.stack([triple(GB - 1), triple(0)])
    owners = jnp.pad(owners, ((0, 16 - GB * GB), (0, 0)))
    gain = norm_gain.reshape(1, C)
    w_mix, w_coarse, w_out = twice(w_mix), twice(w_coarse), twice(w_out)
    double = (2 * C, 2 * C)
    ext = pltpu.VMEM((EXT * EXT * BLK, WIDE), bf16)
    square = (BLK, C)

    (late,) = call(late_kernel, "late_weights", PAIR, [codes, adjacency], [whole(adjacency.shape)],
                   [sds((4 * GB, BLK, SIDE))], [whole((4 * GB, BLK, SIDE))], [], 1 << 20, prefetch=1)
    xu, xd, late, pool, unpool, spread, hot, tails, owners, w_mix, w_coarse, w_out = lax.optimization_barrier((xu, xd, late, pool, unpool, spread, hot, tails, owners, w_mix, w_coarse, w_out))
    early = lambda: [by_step(ROWS)] + [by_step(v.shape[1]) for v in (xu, xd)] + [whole(adjacency.shape)]
    acc, mid = call(
        encode_early, "encode_early", steps, [codes, x, xu, xd, adjacency, gain, w_mix],
        early() + [whole((1, C)), whole(double)],
        [sds((steps, 2 * SIDE, C), ACC), sds((steps, SIDE, C))], [by_step(2 * SIDE), by_step(SIDE)], [ext],
        work * (NB * BLK + C // 3), prefetch=1, exps=work // 6)
    cu, cd = corners(yl, yr, tails)
    halo = lambda: [by_step(v.shape[1]) for v in (yl, yr, cu, cd)]
    tail = lambda v: pl.BlockSpec((1, TAIL, C), lambda p, *_: (0, v.shape[1] // TAIL - 1, 0))
    first_cu, first_cd = cu, cd
    d1, dl, dr, part = call(
        encode_late, "encode_late", steps,
        [x, acc, mid, yl, yr, cu, cd, cu, cd, late, gain, w_mix, w_coarse, pool, unpool, spread, owners],
        [by_step(ROWS), by_step(2 * SIDE), by_step(SIDE)] + halo() + [tail(cu), tail(cd), whole(late.shape)]
        + [whole((1, C)), whole(double), whole(double), whole(pool.shape), whole(unpool.shape), whole(spread.shape), whole(owners.shape)],
        [sds((steps, r, C)) for r in (ROWS, SIDE + TAIL, SIDE + TAIL)] + [sds((devices, steps * C))],
        [by_step(r) for r in (ROWS, SIDE + TAIL, SIDE + TAIL)] + [by_lane(devices)],
        [pltpu.VMEM((ROWS, WIDE), bf16)], work * (C + 3 * crows), exps=work // 3)

    yl = shift(dr, "ry", True)
    yr = shift(dl, "ry", False)
    (part,) = call(part_kernel, "part", PAIR, [part], [whole(part.shape)], [sds(part.shape)], [whole(part.shape)], [], HINT, vmem=4)
    part = part.reshape(devices, 2, steps * C // 2)
    (acc,) = call(decode_early, "decode_early", steps, [codes, d1, adjacency], [by_step(ROWS), whole(adjacency.shape)],
                  [sds((steps, ROWS, C), ACC)], [by_step(ROWS)], [ext], work * NB * BLK, prefetch=1)
    xu, xd, top = rows_halo(d1, 1)
    half = (devices, 2, steps * C // 2)
    arrived = lax.all_to_all(part, ("rx", "ry"), split_axis=0, concat_axis=0, tiled=True)
    region = (jnp.sum(arrived.astype(f32), axis=0, keepdims=True) / float(crows)).astype(bf16)
    everyone = jnp.broadcast_to(region, half)
    everyone, _ = lax.optimization_barrier((everyone, xu))
    region = lax.all_to_all(everyone, ("rx", "ry"), split_axis=0, concat_axis=0, tiled=True)
    region = region.reshape(devices, steps * C)
    yl, yr, _, _ = lax.optimization_barrier((yl, yr, acc, everyone))
    cu, cd = corners(yl, yr, tails)
    (mown,) = call(owners_kernel, "owner_mix", PAIR, [codes, adjacency, owners, first_cu, first_cd, yl, yr],
                   [whole(adjacency.shape), whole(owners.shape)] + [tail(v) for v in (first_cu, first_cd, yl, yr)],
                   [sds((GB * GB,) + square)], [whole((GB * GB,) + square)],
                   [pltpu.VMEM((EXT * EXT * BLK, C), bf16)], HINT, prefetch=1)
    (out,) = call(
        decode_late, "decode_late", steps, [d1, acc, yl, yr, cu, cd, xu, xd, late, mown, region, w_region, w_out, hot],
        [by_step(ROWS)] * 2 + halo() + [by_step(SIDE)] * 2 + [whole(late.shape)]
        + [whole(mown.shape), by_lane(devices), whole(square), whole(double), whole(hot.shape)],
        [sds((steps, ROWS, C))], [by_step(ROWS)], [], work * 3 * C, exps=work // 2, vmem=60)
    return out.transpose(1, 0, 2)


def solution(mesh):
    nodes = P(("rx", "ry"))
    in_specs = (
        P(("rx", "ry"), None, None),
        P(("rx", "ry"), None, None, None),
        P(("rx", "ry"), None),
        P(),
        P(),
        nodes,
        nodes,
        P(("rx", "ry"), None),
        P(),
        P(),
        P(),
    )
    out_specs = P(("rx", "ry"), None, None)
    return jax.shard_map(on_device, mesh=mesh, in_specs=in_specs, out_specs=out_specs, check_vma=False)
```

```python
import functools
import jax
import jax.numpy as jnp
from jax import lax
from jax.experimental import pallas as pl
from jax.experimental.pallas import tpu as pltpu
from jax.sharding import PartitionSpec as P

GB, BLK, NB, C = 3, 128, 6, 128
EXT = GB + 2
ROWS = GB * GB * BLK
SIDE = GB * BLK
PAIR = 6
WIDE = PAIR * C
bf16, f32 = jnp.bfloat16, jnp.float32
ACC = bf16


def silu(v):
    return v / (1.0 + jnp.exp(-v))


def dot(a, b):
    return jnp.dot(a, b, preferred_element_type=f32)


def span(k):
    return slice(k * BLK, (k + 1) * BLK)


def ext_row(codes, j, n):
    code = codes[j * NB + n]
    e = (j // GB + code // 3) * EXT + j % GB + code % 3
    return pl.ds(pl.multiple_of(e * BLK, BLK), BLK)


def fill(ext, own, xu=None, xd=None):
    @pl.when(pl.program_id(0) == 0)
    def _():
        if xu is None:
            ext[...] = jnp.zeros(ext.shape, bf16)
        for e in range(EXT):
            ext[span(e * EXT), :] = jnp.zeros((BLK, WIDE), bf16)
            ext[span(e * EXT + EXT - 1), :] = jnp.zeros((BLK, WIDE), bf16)

    for s in range(PAIR):
        lanes = span(s)

        def put(row, col, block):
            ext[span(row * EXT + col), lanes] = block

        for a in range(GB):
            for b in range(GB):
                put(a + 1, b + 1, own[s, span(a * GB + b), :])
            if xu is not None:
                put(0, a + 1, xu[s, span(a), :])
                put(EXT - 1, a + 1, xd[s, span(a), :])


def early_sum(codes, adj, ext, j):
    weights = jnp.concatenate([adj[j, n] for n in range(NB)], axis=1)
    feats = jnp.concatenate([ext[ext_row(codes, j, n), :] for n in range(NB)], axis=0)
    return dot(weights, feats)


def side_term(late, j, columns):
    a, side = j // GB, int(j % GB > 0)
    return late[side * GB + a], columns[side][a * BLK : (a + GB) * BLK, :]


def row_term(late, j, rows):
    b, low = j % GB, int(j >= GB)
    first, last = max(b - 1, 0), min(b + 1, GB - 1)
    lanes = slice((first - b + 1) * BLK, (last - b + 2) * BLK)
    return late[(2 + low) * GB + b][:, lanes], rows[low][first * BLK : (last + 1) * BLK, :]


def side_columns(yl, yr, cu, cd):
    return [jnp.concatenate([joined(cu, k)] + [joined(y, a) for a in range(GB)] + [joined(cd, k)], axis=0)
            for k, y in enumerate((yl, yr))]


def joined(ref, k):
    return jnp.concatenate([ref[s, span(k), :] for s in range(PAIR)], axis=1)


def twice(w):
    zero = jnp.zeros((C, C), bf16)
    return jnp.concatenate([jnp.concatenate([w, zero], axis=1), jnp.concatenate([zero, w], axis=1)], axis=0)


def mix(values, w):
    parts = [dot(jnp.concatenate(values[s : s + 2], axis=1), w[...]) for s in range(0, PAIR, 2)]
    return [silu(parts[s // 2][:, span(s % 2)]) for s in range(PAIR)]


def norm(diffused, gain):
    v = diffused.astype(bf16).astype(f32)
    ms = jnp.mean(v * v, axis=1, keepdims=True)
    return (v * lax.rsqrt(ms + 1e-6) * gain[...]).astype(bf16)


def mix_in(diffused, own, j, gain, w_mix):
    mixed = mix([norm(v, gain) for v in diffused], w_mix)
    return [(own[s, span(j), :].astype(f32) + mixed[s]).astype(bf16) for s in range(PAIR)]


def encode_early(codes, own, xu, xd, adj, gain, w_mix, acc, mid, ext):
    fill(ext, own, xu, xd)
    for j in range(GB * GB):
        total = early_sum(codes, adj, ext, j)
        a, b = j // GB, j % GB
        parts = [total[:, span(s)] for s in range(PAIR)]
        if b == 1:
            parts = mix_in(parts, own, j, gain, w_mix)
        for s in range(PAIR):
            if b == 1:
                mid[s, span(a), :] = parts[s]
            else:
                acc[s, span(a if b == 0 else GB + a), :] = parts[s].astype(ACC)


def encode_late(own, acc, mid, yl, yr, cu, cd, cut, cdt, late, gain, w_mix, w_coarse, pool, unpool, spread, owners,
                d1, dl, dr, part, enc):
    columns = side_columns(yl, yr, cu, cd)
    for j in range(GB * GB):
        a, b = j // GB, j % GB
        if b == 1:
            for s in range(PAIR):
                enc[span(j), span(s)] = mid[s, span(a), :]
            continue
        rest = dot(*side_term(late, j, columns))
        parts = [acc[s, span(a if b == 0 else GB + a), :] + rest[:, span(s)] for s in range(PAIR)]
        for s, v in enumerate(mix_in(parts, own, j, gain, w_mix)):
            enc[span(j), span(s)] = v
    pooled = dot(pool[...], enc[...]).astype(bf16)
    lifted = jnp.concatenate(mix([pooled[:, span(s)] for s in range(PAIR)], w_coarse), axis=1).astype(bf16)
    part[...] = dot(spread[...], lifted).astype(bf16)
    refined = (pooled.astype(f32) + lifted.astype(f32)).astype(bf16)
    for s in range(PAIR):
        for k, out in ((0, dl), (GB - 1, dr)):
            ids = [cut[0, k : k + 1, :]] + [owners[a * GB + k : a * GB + k + 1, :] for a in range(GB)]
            ids += [cdt[0, k : k + 1, :], jnp.zeros((TAIL - EXT, C), bf16)]
            out[s, SIDE:, :] = jnp.concatenate([v.astype(f32) for v in ids], axis=0).astype(bf16)
    for j in range(GB * GB):
        a, b = j // GB, j % GB
        back = (enc[span(j), :].astype(f32) + dot(unpool[span(j), :], refined)).astype(bf16)
        for s in range(PAIR):
            v = back[:, span(s)]
            d1[s, span(j), :] = v
            if b != 1:
                (dl if b == 0 else dr)[s, span(a), :] = v


def decode_early(codes, own, adj, acc, ext):
    fill(ext, own)
    for j in range(GB * GB):
        total = early_sum(codes, adj, ext, j)
        for s in range(PAIR):
            acc[s, span(j), :] = total[:, span(s)].astype(ACC)


def decode_late(own, acc, yl, yr, cu, cd, xu, xd, late, mown, region, w_region, w_out, hot, out):
    columns = side_columns(yl, yr, cu, cd)
    rows = [jnp.concatenate([joined(x, b) for b in range(GB)], axis=0) for x in (xu, xd)]
    reach = jnp.concatenate([dot(region[:, span(s)], w_region[...]).astype(bf16) for s in range(PAIR)], axis=1)
    for j in range(GB * GB):
        terms = [(mown[j], reach)]
        if j % GB != 1:
            terms.append(side_term(late, j, columns))
        if j // GB != 1:
            terms.append(row_term(late, j, rows))
        rest = dot(jnp.concatenate([w for w, _ in terms], axis=1), jnp.concatenate([v for _, v in terms], axis=0))
        extra = dot(hot[span(j), :], reach)
        mixed = mix([(acc[s, span(j), :] + rest[:, span(s)]).astype(bf16) for s in range(PAIR)], w_out)
        for s in range(PAIR):
            dec = (own[s, span(j), :].astype(f32) + extra[:, span(s)]).astype(bf16).astype(f32)
            out[s, span(j), :] = (dec + mixed[s]).astype(bf16)


def late_kernel(codes, adj, late):
    for k in range(4 * GB):
        side, a = k // GB % 2, k % GB
        j = a * GB + side * (GB - 1) if k < 2 * GB else side * (GB - 1) * GB + a
        for d in range(GB):
            code = d * GB + side * (GB - 1) if k < 2 * GB else side * (GB - 1) * GB + d
            total = jnp.zeros((BLK, BLK), f32)
            for n in range(NB):
                total += jnp.where(codes[j * NB + n] == code, adj[j, n].astype(f32), 0.0)
            late[k, :, span(d)] = total.astype(bf16)


def owners_kernel(codes, adj, owners, cut, cdt, ylt, yrt, mown, hot):
    ids = lax.broadcasted_iota(jnp.int32, (C, BLK), 0)
    for e in range(EXT * EXT):
        a, b = e // EXT, e % EXT
        if b in (0, EXT - 1):
            row = (yrt if b else ylt)[0, a : a + 1, :]
        elif a in (0, EXT - 1):
            row = (cdt if a else cut)[0, b - 1 : b, :]
        else:
            k = (a - 1) * GB + b - 1
            row = owners[k : k + 1, :]
        row = row.astype(f32).astype(jnp.int32) - 1
        hot[span(e), :] = (ids == row).astype(f32).astype(bf16)
    for j in range(GB * GB):
        acc = jnp.zeros((BLK, C), f32)
        for n in range(NB):
            acc += lax.dot_general(
                adj[j, n], hot[ext_row(codes, j, n), :], (((1,), (1,)), ((), ())), preferred_element_type=f32
            )
        mown[j] = acc.astype(bf16)


def whole(shape):
    return pl.BlockSpec(shape, lambda p, *_: (0,) * len(shape), pipeline_mode=pl.Buffered(1))


def by_step(rows):
    return pl.BlockSpec((PAIR, rows, C), lambda p, *_: (p, 0, 0))


def by_lane(rows):
    return pl.BlockSpec((rows, WIDE), lambda p, *_: (0, p))


def call(kernel, name, steps, args, specs, outs, out_specs, scratch, flops, prefetch=0, exps=0, vmem=None):
    size = lambda v: v.size * v.dtype.itemsize
    return pl.pallas_call(
        kernel,
        grid_spec=pltpu.PrefetchScalarGridSpec(
            num_scalar_prefetch=prefetch, grid=(steps // PAIR,), in_specs=specs, out_specs=out_specs, scratch_shapes=scratch
        ),
        out_shape=outs,
        compiler_params=pltpu.CompilerParams(vmem_limit_bytes=(vmem or VMEM) << 20, dimension_semantics=("arbitrary",)),
        name=name,
        cost_estimate=pl.CostEstimate(
            flops=flops, bytes_accessed=sum(map(size, args)) + sum(map(size, outs)), transcendentals=exps
        ),
    )(*args)


TAIL = 8
HINT = 1 << 34
VMEM = 28


def sds(shape, dtype=bf16):
    return jax.ShapeDtypeStruct(shape, dtype)


def shift(block, axis, up):
    count = lax.axis_size(axis)
    pairs = [(i, i + 1) for i in range(count - 1)]
    return lax.ppermute(block, axis, pairs if up else [(b, a) for a, b in pairs])


def corner_kernel(lt, lb, rt, rb, tails, up, down):
    for out, left, right, k in ((up, lb, rb, 0), (down, lt, rt, 1)):
        out[:, :BLK, :] = left[...]
        out[:, BLK : 2 * BLK, :] = right[...]
        out[:, 2 * BLK :, :] = jnp.broadcast_to(tails[k][None], (out.shape[0], TAIL, C))


def sides_kernel(*refs):
    for k, out in enumerate(refs[-2:]):
        for a in range(GB):
            out[:, span(a), :] = refs[k * GB + a][...]


def sides(x):
    block = lambda k: pl.BlockSpec((PAIR, BLK, C), lambda p, *_: (p, k, 0))
    return call(sides_kernel, "pack_sides", x.shape[0], [x] * (2 * GB),
                [block(a * GB + b) for b in (GB - 1, 0) for a in range(GB)],
                [sds((x.shape[0], SIDE, C))] * 2, [by_step(SIDE)] * 2, [], 1, vmem=60)


def rows_kernel(x, top, bottom):
    top[...] = x[:, :SIDE, :]
    bottom[...] = x[:, ROWS - SIDE :, :]


def rows_halo(x, hint):
    top, bottom = call(rows_kernel, "pack_rows", x.shape[0], [x], [by_step(ROWS)],
                       [sds((x.shape[0], SIDE, C))] * 2, [by_step(SIDE)] * 2, [], hint)
    return shift(bottom, "rx", True), shift(top, "rx", False), top


def corners(yl, yr, tails):
    steps = yl.shape[0]
    block = lambda a: pl.BlockSpec((PAIR, BLK, C), lambda p, *_: (p, a, 0))
    up, down = call(corner_kernel, "pack_corners", steps, [yl, yl, yr, yr, tails],
                    [block(0), block(GB - 1)] * 2 + [whole(tails.shape)],
                    [sds((steps, 2 * BLK + TAIL, C))] * 2, [by_step(2 * BLK + TAIL)] * 2, [], 1, vmem=8)
    return shift(up, "rx", True), shift(down, "rx", False)


def part_kernel(part, out):
    out[...] = part[...]


def on_device(noisy_input, adjacency, neighbours, norm_gain, w_mix, pool_weight, cluster, owner_ids, w_coarse, w_region, w_out):
    steps = noisy_input.shape[1]
    x = noisy_input.transpose(1, 0, 2)
    codes = neighbours.reshape(-1)
    crows = owner_ids.shape[0]
    devices = lax.axis_size("rx") * lax.axis_size("ry")
    squares = x.reshape(steps, GB, GB, BLK, C)
    flat = lambda v: v.reshape(steps, -1, C)
    work = steps * ROWS * C * 2

    owner = owner_ids[:, 0]
    coarse = jnp.arange(crows, dtype=jnp.int32)
    ids = jnp.arange(devices, dtype=jnp.int32)
    hit = cluster[None, :] == coarse[:, None]
    node_owner = jnp.sum(jnp.where(hit, owner[:, None], 0), axis=0)
    owners = (node_owner + 1).astype(bf16).reshape(GB * GB, BLK)

    right, left = sides(x)
    yl = shift(right, "ry", True)
    yr = shift(left, "ry", False)
    x_late, _, _ = lax.optimization_barrier((x, right, left))
    xu, xd, _ = rows_halo(x_late, HINT)
    pool = jnp.where(hit, pool_weight[None, :], jnp.zeros((), bf16))
    unpool = (cluster[:, None] == coarse[None, :]).astype(bf16)
    spread = (owner[None, :] == ids[:, None]).astype(bf16)
    hot = (node_owner[:, None] == ids[None, :]).astype(bf16)
    triple = lambda a: jnp.pad(owners[a * GB : (a + 1) * GB], ((0, TAIL - GB), (0, 0)))
    tails = jnp.stack([triple(GB - 1), triple(0)])
    owners = jnp.pad(owners, ((0, 16 - GB * GB), (0, 0)))
    gain = norm_gain.reshape(1, C)
    w_mix, w_coarse, w_out = twice(w_mix), twice(w_coarse), twice(w_out)
    double = (2 * C, 2 * C)
    ext = pltpu.VMEM((EXT * EXT * BLK, WIDE), bf16)
    square = (BLK, C)

    (late,) = call(late_kernel, "late_weights", PAIR, [codes, adjacency], [whole(adjacency.shape)],
                   [sds((4 * GB, BLK, SIDE))], [whole((4 * GB, BLK, SIDE))], [], 1 << 20, prefetch=1)
    xu, xd, late, pool, unpool, spread, hot, tails, owners, w_mix, w_coarse, w_out = lax.optimization_barrier((xu, xd, late, pool, unpool, spread, hot, tails, owners, w_mix, w_coarse, w_out))
    early = lambda: [by_step(ROWS)] + [by_step(v.shape[1]) for v in (xu, xd)] + [whole(adjacency.shape)]
    acc, mid = call(
        encode_early, "encode_early", steps, [codes, x, xu, xd, adjacency, gain, w_mix],
        early() + [whole((1, C)), whole(double)],
        [sds((steps, 2 * SIDE, C), ACC), sds((steps, SIDE, C))], [by_step(2 * SIDE), by_step(SIDE)], [ext],
        work * (NB * BLK + C // 3), prefetch=1, exps=work // 6)
    cu, cd = corners(yl, yr, tails)
    halo = lambda: [by_step(v.shape[1]) for v in (yl, yr, cu, cd)]
    tail = lambda v: pl.BlockSpec((1, TAIL, C), lambda p, *_: (0, v.shape[1] // TAIL - 1, 0))
    first_cu, first_cd = cu, cd
    d1, dl, dr, part = call(
        encode_late, "encode_late", steps,
        [x, acc, mid, yl, yr, cu, cd, cu, cd, late, gain, w_mix, w_coarse, pool, unpool, spread, owners],
        [by_step(ROWS), by_step(2 * SIDE), by_step(SIDE)] + halo() + [tail(cu), tail(cd), whole(late.shape)]
        + [whole((1, C)), whole(double), whole(double), whole(pool.shape), whole(unpool.shape), whole(spread.shape), whole(owners.shape)],
        [sds((steps, r, C)) for r in (ROWS, SIDE + TAIL, SIDE + TAIL)] + [sds((devices, steps * C))],
        [by_step(r) for r in (ROWS, SIDE + TAIL, SIDE + TAIL)] + [by_lane(devices)],
        [pltpu.VMEM((ROWS, WIDE), bf16)], work * (C + 3 * crows), exps=work // 3)

    yl = shift(dr, "ry", True)
    yr = shift(dl, "ry", False)
    (part,) = call(part_kernel, "part", PAIR, [part], [whole(part.shape)], [sds(part.shape)], [whole(part.shape)], [], HINT, vmem=4)
    part = part.reshape(devices, 2, steps * C // 2)
    (acc,) = call(decode_early, "decode_early", steps, [codes, d1, adjacency], [by_step(ROWS), whole(adjacency.shape)],
                  [sds((steps, ROWS, C), ACC)], [by_step(ROWS)], [ext], work * NB * BLK, prefetch=1, vmem=60)
    xu, xd, top = rows_halo(d1, 1)
    half = (devices, 2, steps * C // 2)
    arrived = lax.all_to_all(part, ("rx", "ry"), split_axis=0, concat_axis=0, tiled=True)
    region = (jnp.sum(arrived.astype(f32), axis=0, keepdims=True) / float(crows)).astype(bf16)
    everyone = jnp.broadcast_to(region, half)
    everyone, _ = lax.optimization_barrier((everyone, xu))
    region = lax.all_to_all(everyone, ("rx", "ry"), split_axis=0, concat_axis=0, tiled=True)
    region = region.reshape(devices, steps * C)
    yl, yr, _, _ = lax.optimization_barrier((yl, yr, acc, everyone))
    cu, cd = corners(yl, yr, tails)
    (mown,) = call(owners_kernel, "owner_mix", PAIR, [codes, adjacency, owners, first_cu, first_cd, yl, yr],
                   [whole(adjacency.shape), whole(owners.shape)] + [tail(v) for v in (first_cu, first_cd, yl, yr)],
                   [sds((GB * GB,) + square)], [whole((GB * GB,) + square)],
                   [pltpu.VMEM((EXT * EXT * BLK, C), bf16)], HINT, prefetch=1)
    (out,) = call(
        decode_late, "decode_late", steps, [d1, acc, yl, yr, cu, cd, xu, xd, late, mown, region, w_region, w_out, hot],
        [by_step(ROWS)] * 2 + halo() + [by_step(SIDE)] * 2 + [whole(late.shape)]
        + [whole(mown.shape), by_lane(devices), whole(square), whole(double), whole(hot.shape)],
        [sds((steps, ROWS, C))], [by_step(ROWS)], [], work * 3 * C, exps=work // 2, vmem=60)
    return out.transpose(1, 0, 2)


def solution(mesh):
    nodes = P(("rx", "ry"))
    in_specs = (
        P(("rx", "ry"), None, None),
        P(("rx", "ry"), None, None, None),
        P(("rx", "ry"), None),
        P(),
        P(),
        nodes,
        nodes,
        P(("rx", "ry"), None),
        P(),
        P(),
        P(),
    )
    out_specs = P(("rx", "ry"), None, None)
    return jax.shard_map(on_device, mesh=mesh, in_specs=in_specs, out_specs=out_specs, check_vma=False)
```

```python
import functools
import jax
import jax.numpy as jnp
from jax import lax
from jax.experimental import pallas as pl
from jax.experimental.pallas import tpu as pltpu
from jax.sharding import PartitionSpec as P

GB, BLK, NB, C = 3, 128, 6, 128
EXT = GB + 2
ROWS = GB * GB * BLK
SIDE = GB * BLK
PAIR = 6
WIDE = PAIR * C
bf16, f32 = jnp.bfloat16, jnp.float32
ACC = bf16


def silu(v):
    return v / (1.0 + jnp.exp(-v))


def dot(a, b):
    return jnp.dot(a, b, preferred_element_type=f32)


def span(k):
    return slice(k * BLK, (k + 1) * BLK)


def ext_row(codes, j, n):
    code = codes[j * NB + n]
    e = (j // GB + code // 3) * EXT + j % GB + code % 3
    return pl.ds(pl.multiple_of(e * BLK, BLK), BLK)


def fill(ext, own, xu=None, xd=None):
    @pl.when(pl.program_id(0) == 0)
    def _():
        if xu is None:
            ext[...] = jnp.zeros(ext.shape, bf16)
        for e in range(EXT):
            ext[span(e * EXT), :] = jnp.zeros((BLK, WIDE), bf16)
            ext[span(e * EXT + EXT - 1), :] = jnp.zeros((BLK, WIDE), bf16)

    for s in range(PAIR):
        lanes = span(s)

        def put(row, col, block):
            ext[span(row * EXT + col), lanes] = block

        for a in range(GB):
            for b in range(GB):
                put(a + 1, b + 1, own[s, span(a * GB + b), :])
            if xu is not None:
                put(0, a + 1, xu[s, span(a), :])
                put(EXT - 1, a + 1, xd[s, span(a), :])


def early_sum(codes, adj, ext, j):
    weights = jnp.concatenate([adj[j, n] for n in range(NB)], axis=1)
    feats = jnp.concatenate([ext[ext_row(codes, j, n), :] for n in range(NB)], axis=0)
    return dot(weights, feats)


def side_term(late, j, columns):
    a, side = j // GB, int(j % GB > 0)
    return late[side * GB + a], columns[side][a * BLK : (a + GB) * BLK, :]


def row_term(late, j, rows):
    b, low = j % GB, int(j >= GB)
    first, last = max(b - 1, 0), min(b + 1, GB - 1)
    lanes = slice((first - b + 1) * BLK, (last - b + 2) * BLK)
    return late[(2 + low) * GB + b][:, lanes], rows[low][first * BLK : (last + 1) * BLK, :]


def side_columns(yl, yr, cu, cd):
    return [jnp.concatenate([joined(cu, k)] + [joined(y, a) for a in range(GB)] + [joined(cd, k)], axis=0)
            for k, y in enumerate((yl, yr))]


def joined(ref, k):
    return jnp.concatenate([ref[s, span(k), :] for s in range(PAIR)], axis=1)


def twice(w):
    zero = jnp.zeros((C, C), bf16)
    return jnp.concatenate([jnp.concatenate([w, zero], axis=1), jnp.concatenate([zero, w], axis=1)], axis=0)


def mix(values, w):
    parts = [dot(jnp.concatenate(values[s : s + 2], axis=1), w[...]) for s in range(0, PAIR, 2)]
    return [silu(parts[s // 2][:, span(s % 2)]) for s in range(PAIR)]


def norm(diffused, gain):
    v = diffused.astype(bf16).astype(f32)
    ms = jnp.mean(v * v, axis=1, keepdims=True)
    return (v * lax.rsqrt(ms + 1e-6) * gain[...]).astype(bf16)


def mix_in(diffused, own, j, gain, w_mix):
    mixed = mix([norm(v, gain) for v in diffused], w_mix)
    return [(own[s, span(j), :].astype(f32) + mixed[s]).astype(bf16) for s in range(PAIR)]


def encode_early(codes, own, xu, xd, adj, gain, w_mix, acc, mid, ext):
    fill(ext, own, xu, xd)
    for j in range(GB * GB):
        total = early_sum(codes, adj, ext, j)
        a, b = j // GB, j % GB
        parts = [total[:, span(s)] for s in range(PAIR)]
        if b == 1:
            parts = mix_in(parts, own, j, gain, w_mix)
        for s in range(PAIR):
            if b == 1:
                mid[s, span(a), :] = parts[s]
            else:
                acc[s, span(a if b == 0 else GB + a), :] = parts[s].astype(ACC)


def encode_late(own, acc, mid, yl, yr, cu, cd, cut, cdt, late, gain, w_mix, w_coarse, pool, unpool, spread, owners,
                d1, dl, dr, part, enc):
    columns = side_columns(yl, yr, cu, cd)
    for j in range(GB * GB):
        a, b = j // GB, j % GB
        if b == 1:
            for s in range(PAIR):
                enc[span(j), span(s)] = mid[s, span(a), :]
            continue
        rest = dot(*side_term(late, j, columns))
        parts = [acc[s, span(a if b == 0 else GB + a), :] + rest[:, span(s)] for s in range(PAIR)]
        for s, v in enumerate(mix_in(parts, own, j, gain, w_mix)):
            enc[span(j), span(s)] = v
    pooled = dot(pool[...], enc[...]).astype(bf16)
    lifted = jnp.concatenate(mix([pooled[:, span(s)] for s in range(PAIR)], w_coarse), axis=1).astype(bf16)
    part[...] = dot(spread[...], lifted).astype(bf16)
    refined = (pooled.astype(f32) + lifted.astype(f32)).astype(bf16)
    for s in range(PAIR):
        for k, out in ((0, dl), (GB - 1, dr)):
            ids = [cut[0, k : k + 1, :]] + [owners[a * GB + k : a * GB + k + 1, :] for a in range(GB)]
            ids += [cdt[0, k : k + 1, :], jnp.zeros((TAIL - EXT, C), bf16)]
            out[s, SIDE:, :] = jnp.concatenate([v.astype(f32) for v in ids], axis=0).astype(bf16)
    for j in range(GB * GB):
        a, b = j // GB, j % GB
        back = (enc[span(j), :].astype(f32) + dot(unpool[span(j), :], refined)).astype(bf16)
        for s in range(PAIR):
            v = back[:, span(s)]
            d1[s, span(j), :] = v
            if b != 1:
                (dl if b == 0 else dr)[s, span(a), :] = v


def decode_early(codes, own, adj, acc, ext):
    fill(ext, own)
    for j in range(GB * GB):
        total = early_sum(codes, adj, ext, j)
        for s in range(PAIR):
            acc[s, span(j), :] = total[:, span(s)].astype(ACC)


def decode_late(own, acc, yl, yr, cu, cd, xu, xd, late, mown, region, w_region, w_out, hot, out):
    columns = side_columns(yl, yr, cu, cd)
    rows = [jnp.concatenate([joined(x, b) for b in range(GB)], axis=0) for x in (xu, xd)]
    reach = jnp.concatenate([dot(region[:, span(s)], w_region[...]).astype(bf16) for s in range(PAIR)], axis=1)
    for j in range(GB * GB):
        terms = [(mown[j], reach)]
        if j % GB != 1:
            terms.append(side_term(late, j, columns))
        if j // GB != 1:
            terms.append(row_term(late, j, rows))
        rest = dot(jnp.concatenate([w for w, _ in terms], axis=1), jnp.concatenate([v for _, v in terms], axis=0))
        extra = dot(hot[span(j), :], reach)
        mixed = mix([(acc[s, span(j), :] + rest[:, span(s)]).astype(bf16) for s in range(PAIR)], w_out)
        for s in range(PAIR):
            dec = (own[s, span(j), :].astype(f32) + extra[:, span(s)]).astype(bf16).astype(f32)
            out[s, span(j), :] = (dec + mixed[s]).astype(bf16)


def late_kernel(codes, adj, late):
    for k in range(4 * GB):
        side, a = k // GB % 2, k % GB
        j = a * GB + side * (GB - 1) if k < 2 * GB else side * (GB - 1) * GB + a
        for d in range(GB):
            code = d * GB + side * (GB - 1) if k < 2 * GB else side * (GB - 1) * GB + d
            total = jnp.zeros((BLK, BLK), f32)
            for n in range(NB):
                total += jnp.where(codes[j * NB + n] == code, adj[j, n].astype(f32), 0.0)
            late[k, :, span(d)] = total.astype(bf16)


def owners_kernel(codes, adj, owners, cut, cdt, ylt, yrt, mown, hot):
    ids = lax.broadcasted_iota(jnp.int32, (C, BLK), 0)
    for e in range(EXT * EXT):
        a, b = e // EXT, e % EXT
        if b in (0, EXT - 1):
            row = (yrt if b else ylt)[0, a : a + 1, :]
        elif a in (0, EXT - 1):
            row = (cdt if a else cut)[0, b - 1 : b, :]
        else:
            k = (a - 1) * GB + b - 1
            row = owners[k : k + 1, :]
        row = row.astype(f32).astype(jnp.int32) - 1
        hot[span(e), :] = (ids == row).astype(f32).astype(bf16)
    for j in range(GB * GB):
        acc = jnp.zeros((BLK, C), f32)
        for n in range(NB):
            acc += lax.dot_general(
                adj[j, n], hot[ext_row(codes, j, n), :], (((1,), (1,)), ((), ())), preferred_element_type=f32
            )
        mown[j] = acc.astype(bf16)


def whole(shape):
    return pl.BlockSpec(shape, lambda p, *_: (0,) * len(shape), pipeline_mode=pl.Buffered(1))


def by_step(rows):
    return pl.BlockSpec((PAIR, rows, C), lambda p, *_: (p, 0, 0))


def by_lane(rows):
    return pl.BlockSpec((rows, WIDE), lambda p, *_: (0, p))


def call(kernel, name, steps, args, specs, outs, out_specs, scratch, flops, prefetch=0, exps=0, vmem=None):
    size = lambda v: v.size * v.dtype.itemsize
    return pl.pallas_call(
        kernel,
        grid_spec=pltpu.PrefetchScalarGridSpec(
            num_scalar_prefetch=prefetch, grid=(steps // PAIR,), in_specs=specs, out_specs=out_specs, scratch_shapes=scratch
        ),
        out_shape=outs,
        compiler_params=pltpu.CompilerParams(vmem_limit_bytes=(vmem or VMEM) << 20, dimension_semantics=("arbitrary",)),
        name=name,
        cost_estimate=pl.CostEstimate(
            flops=flops, bytes_accessed=sum(map(size, args)) + sum(map(size, outs)), transcendentals=exps
        ),
    )(*args)


TAIL = 8
HINT = 1 << 34
VMEM = 28


def sds(shape, dtype=bf16):
    return jax.ShapeDtypeStruct(shape, dtype)


def shift(block, axis, up):
    count = lax.axis_size(axis)
    pairs = [(i, i + 1) for i in range(count - 1)]
    return lax.ppermute(block, axis, pairs if up else [(b, a) for a, b in pairs])


def corner_kernel(lt, lb, rt, rb, tails, up, down):
    for out, left, right, k in ((up, lb, rb, 0), (down, lt, rt, 1)):
        out[:, :BLK, :] = left[...]
        out[:, BLK : 2 * BLK, :] = right[...]
        out[:, 2 * BLK :, :] = jnp.broadcast_to(tails[k][None], (out.shape[0], TAIL, C))


def sides_kernel(*refs):
    for k, out in enumerate(refs[-2:]):
        for a in range(GB):
            out[:, span(a), :] = refs[k * GB + a][...]


def sides(x):
    block = lambda k: pl.BlockSpec((2, BLK, C), lambda p, *_: (p, k, 0))
    return call(sides_kernel, "pack_sides", x.shape[0] // 2 * PAIR, [x] * (2 * GB),
                [block(a * GB + b) for b in (GB - 1, 0) for a in range(GB)],
                [sds((x.shape[0], SIDE, C))] * 2, [pl.BlockSpec((2, SIDE, C), lambda p, *_: (p, 0, 0))] * 2, [], 1, vmem=60)


def rows_kernel(x, top, bottom):
    top[...] = x[:, :SIDE, :]
    bottom[...] = x[:, ROWS - SIDE :, :]


def rows_halo(x, hint):
    top, bottom = call(rows_kernel, "pack_rows", x.shape[0], [x], [by_step(ROWS)],
                       [sds((x.shape[0], SIDE, C))] * 2, [by_step(SIDE)] * 2, [], hint)
    return shift(bottom, "rx", True), shift(top, "rx", False), top


def corners(yl, yr, tails):
    steps = yl.shape[0]
    block = lambda a: pl.BlockSpec((PAIR, BLK, C), lambda p, *_: (p, a, 0))
    up, down = call(corner_kernel, "pack_corners", steps, [yl, yl, yr, yr, tails],
                    [block(0), block(GB - 1)] * 2 + [whole(tails.shape)],
                    [sds((steps, 2 * BLK + TAIL, C))] * 2, [by_step(2 * BLK + TAIL)] * 2, [], 1, vmem=8)
    return shift(up, "rx", True), shift(down, "rx", False)


def part_kernel(part, out):
    out[...] = part[...]


def on_device(noisy_input, adjacency, neighbours, norm_gain, w_mix, pool_weight, cluster, owner_ids, w_coarse, w_region, w_out):
    steps = noisy_input.shape[1]
    x = noisy_input.transpose(1, 0, 2)
    codes = neighbours.reshape(-1)
    crows = owner_ids.shape[0]
    devices = lax.axis_size("rx") * lax.axis_size("ry")
    squares = x.reshape(steps, GB, GB, BLK, C)
    flat = lambda v: v.reshape(steps, -1, C)
    work = steps * ROWS * C * 2

    owner = owner_ids[:, 0]
    coarse = jnp.arange(crows, dtype=jnp.int32)
    ids = jnp.arange(devices, dtype=jnp.int32)
    hit = cluster[None, :] == coarse[:, None]
    node_owner = jnp.sum(jnp.where(hit, owner[:, None], 0), axis=0)
    owners = (node_owner + 1).astype(bf16).reshape(GB * GB, BLK)

    right, left = sides(x)
    yl = shift(right, "ry", True)
    yr = shift(left, "ry", False)
    x_late, _, _ = lax.optimization_barrier((x, right, left))
    xu, xd, _ = rows_halo(x_late, HINT)
    pool = jnp.where(hit, pool_weight[None, :], jnp.zeros((), bf16))
    unpool = (cluster[:, None] == coarse[None, :]).astype(bf16)
    spread = (owner[None, :] == ids[:, None]).astype(bf16)
    hot = (node_owner[:, None] == ids[None, :]).astype(bf16)
    triple = lambda a: jnp.pad(owners[a * GB : (a + 1) * GB], ((0, TAIL - GB), (0, 0)))
    tails = jnp.stack([triple(GB - 1), triple(0)])
    owners = jnp.pad(owners, ((0, 16 - GB * GB), (0, 0)))
    gain = norm_gain.reshape(1, C)
    w_mix, w_coarse, w_out = twice(w_mix), twice(w_coarse), twice(w_out)
    double = (2 * C, 2 * C)
    ext = pltpu.VMEM((EXT * EXT * BLK, WIDE), bf16)
    square = (BLK, C)

    (late,) = call(late_kernel, "late_weights", PAIR, [codes, adjacency], [whole(adjacency.shape)],
                   [sds((4 * GB, BLK, SIDE))], [whole((4 * GB, BLK, SIDE))], [], 1 << 20, prefetch=1)
    xu, xd, late, pool, unpool, spread, hot, tails, owners, w_mix, w_coarse, w_out = lax.optimization_barrier((xu, xd, late, pool, unpool, spread, hot, tails, owners, w_mix, w_coarse, w_out))
    early = lambda: [by_step(ROWS)] + [by_step(v.shape[1]) for v in (xu, xd)] + [whole(adjacency.shape)]
    acc, mid = call(
        encode_early, "encode_early", steps, [codes, x, xu, xd, adjacency, gain, w_mix],
        early() + [whole((1, C)), whole(double)],
        [sds((steps, 2 * SIDE, C), ACC), sds((steps, SIDE, C))], [by_step(2 * SIDE), by_step(SIDE)], [ext],
        work * (NB * BLK + C // 3), prefetch=1, exps=work // 6)
    cu, cd = corners(yl, yr, tails)
    halo = lambda: [by_step(v.shape[1]) for v in (yl, yr, cu, cd)]
    tail = lambda v: pl.BlockSpec((1, TAIL, C), lambda p, *_: (0, v.shape[1] // TAIL - 1, 0))
    first_cu, first_cd = cu, cd
    d1, dl, dr, part = call(
        encode_late, "encode_late", steps,
        [x, acc, mid, yl, yr, cu, cd, cu, cd, late, gain, w_mix, w_coarse, pool, unpool, spread, owners],
        [by_step(ROWS), by_step(2 * SIDE), by_step(SIDE)] + halo() + [tail(cu), tail(cd), whole(late.shape)]
        + [whole((1, C)), whole(double), whole(double), whole(pool.shape), whole(unpool.shape), whole(spread.shape), whole(owners.shape)],
        [sds((steps, r, C)) for r in (ROWS, SIDE + TAIL, SIDE + TAIL)] + [sds((devices, steps * C))],
        [by_step(r) for r in (ROWS, SIDE + TAIL, SIDE + TAIL)] + [by_lane(devices)],
        [pltpu.VMEM((ROWS, WIDE), bf16)], work * (C + 3 * crows), exps=work // 3)

    yl = shift(dr, "ry", True)
    yr = shift(dl, "ry", False)
    (part,) = call(part_kernel, "part", PAIR, [part], [whole(part.shape)], [sds(part.shape)], [whole(part.shape)], [], HINT, vmem=4)
    part = part.reshape(devices, 2, steps * C // 2)
    (acc,) = call(decode_early, "decode_early", steps, [codes, d1, adjacency], [by_step(ROWS), whole(adjacency.shape)],
                  [sds((steps, ROWS, C), ACC)], [by_step(ROWS)], [ext], work * NB * BLK, prefetch=1, vmem=60)
    xu, xd, top = rows_halo(d1, 1)
    half = (devices, 2, steps * C // 2)
    arrived = lax.all_to_all(part, ("rx", "ry"), split_axis=0, concat_axis=0, tiled=True)
    region = (jnp.sum(arrived.astype(f32), axis=0, keepdims=True) / float(crows)).astype(bf16)
    everyone = jnp.broadcast_to(region, half)
    everyone, _ = lax.optimization_barrier((everyone, xu))
    region = lax.all_to_all(everyone, ("rx", "ry"), split_axis=0, concat_axis=0, tiled=True)
    region = region.reshape(devices, steps * C)
    yl, yr, _, _ = lax.optimization_barrier((yl, yr, acc, everyone))
    cu, cd = corners(yl, yr, tails)
    (mown,) = call(owners_kernel, "owner_mix", PAIR, [codes, adjacency, owners, first_cu, first_cd, yl, yr],
                   [whole(adjacency.shape), whole(owners.shape)] + [tail(v) for v in (first_cu, first_cd, yl, yr)],
                   [sds((GB * GB,) + square)], [whole((GB * GB,) + square)],
                   [pltpu.VMEM((EXT * EXT * BLK, C), bf16)], HINT, prefetch=1)
    (out,) = call(
        decode_late, "decode_late", steps, [d1, acc, yl, yr, cu, cd, xu, xd, late, mown, region, w_region, w_out, hot],
        [by_step(ROWS)] * 2 + halo() + [by_step(SIDE)] * 2 + [whole(late.shape)]
        + [whole(mown.shape), by_lane(devices), whole(square), whole(double), whole(hot.shape)],
        [sds((steps, ROWS, C))], [by_step(ROWS)], [], work * 3 * C, exps=work // 2, vmem=60)
    return out.transpose(1, 0, 2)


def solution(mesh):
    nodes = P(("rx", "ry"))
    in_specs = (
        P(("rx", "ry"), None, None),
        P(("rx", "ry"), None, None, None),
        P(("rx", "ry"), None),
        P(),
        P(),
        nodes,
        nodes,
        P(("rx", "ry"), None),
        P(),
        P(),
        P(),
    )
    out_specs = P(("rx", "ry"), None, None)
    return jax.shard_map(on_device, mesh=mesh, in_specs=in_specs, out_specs=out_specs, check_vma=False)
```
